128 devices in a mesh: sec: 2 (over y_lo), dev: 64 (over x, y_hi, z, core).
Axes of the slice: x: 4, y: 4 (y_hi: 2, y_lo: 2; y = y_hi * 2 + y_lo), z: 4, core: 2. Of those that a mesh axis runs over, the one named last changes fastest.
Arguments:
- hidden_in: bfloat16 [2048, 7168], P(('sec', 'dev')), may hold values from -6 to 6
- expert_ids: int32 [2048, 8], P(('sec', 'dev')), may hold values from 0 to 63, all different within a row; in each aligned block of 8 rows (0 to 7, 8 to 15, ...) at most 2 rows name the same one
- gate_coef: float32 [2048, 8], P(('sec', 'dev')), may hold values from 0.1 to 1
- query_lat: bfloat16 [2048, 64, 576], P(('sec', 'dev')), may hold values from -40 to 40
- kv_cache: bfloat16 [2048, 128, 576], P(('sec', 'dev')), may hold values from -6 to 6
- cache_len: int32 [2048], P(('sec', 'dev')), may hold values from 32 to 128, as said below
- gate_weight: bfloat16 [64, 7168, 1024], P('dev', None, 'sec'), may hold values from -0.0625 to 0.0625
- up_weight: bfloat16 [64, 7168, 1024], P('dev', None, 'sec'), may hold values from -0.0625 to 0.0625
- down_weight: bfloat16 [64, 1024, 7168], P('dev', 'sec'), may hold values from -0.1875 to 0.1875
Outputs:
- attention: bfloat16 [2048, 64, 512], P(('sec', 'dev'))
- routed_out: bfloat16 [2048, 7168], P(('sec', 'dev'))
The draws below stay inside these ranges and needn't reach their ends.
Inputs may be any that keep to these rules, and one draw needn't show every extreme that they name: `expert_ids`: each row names 8 different experts. In each aligned block of 8 rows (one micro-batch of one device) no expert is named by more than 2 rows, and in some block an expert is named by exactly 2 rows. `cache_len`: some row uses all 128 slots.
All inputs are finite; a program needn't handle non-finite values.
Results may differ from the reference program's by a relative error of at most 0.0065.
Values may be sent and summed in bfloat16 or wider, within the bound.
A program may use at most 128 MiB of HBM per device.

```python
import math
import jax
import jax.numpy as jnp
import numpy as np
from jax import lax

D = 7168
FF = 1024
HEADS = 64
LAT = 512
ROPE = 64
TOP = 8
CTX = 128
MB_ROWS = 8
ROWS = 2048
EXPERTS = 64
CAP = 2
N_SEC = 2


def latent_pair(key):
    base = jax.random.fold_in(key, 7)
    keys = jax.random.split(base, 2)
    width = LAT + ROPE
    cache_vals = jnp.clip(jax.random.normal(keys[0], (ROWS, CTX, width), jnp.float32), -5.0, 5.0)
    query_vals = jnp.clip(jax.random.normal(keys[1], (ROWS, HEADS, width), jnp.float32), -5.0, 5.0)
    return (cache_vals, query_vals)


def draw_query_lat(key, part):
    cache_vals, query_vals = latent_pair(key)
    return query_vals.astype(jnp.bfloat16)


def draw_kv_cache(key, part):
    cache_vals, query_vals = latent_pair(key)
    return cache_vals.astype(jnp.bfloat16)


def draw_cache_len(key, part):
    keys = jax.random.split(jax.random.fold_in(key, 11), 2)
    lengths = jax.random.randint(keys[0], (ROWS,), CTX // 4, CTX + 1)
    full_row = jax.random.randint(keys[1], (), 0, ROWS)
    return jnp.where(jnp.arange(ROWS) == full_row, CTX, lengths).astype(jnp.int32)


def steps_of(rng, extent, cuts, least, top_value):
    def one(position, shards_of):
        heights = jax.random.uniform(jax.random.fold_in(jax.random.fold_in(rng, 6), position), (shards_of,), jnp.float32, least / len(cuts), top_value / len(cuts))
        return jnp.repeat(jnp.exp(heights), extent[position] // shards_of).reshape((-1,) + (1,) * (len(extent) - position - 1))

    factor_of = one(*cuts[0])
    for cut in cuts[1:]:
        factor_of = factor_of * one(*cut)
    return factor_of


def routed_block(key, own, number, rows, amount, top, most, slope):
    sequence = jax.random.permutation(key, amount)
    crowded, ordinary = shares(amount, rows * top, most, slope, True), shares(amount, rows * top, most, slope, False)
    places = jnp.arange(amount)

    def named(sizes, turn):
        used = int((sizes > 0).sum())
        fixed = max(1, used // 4)
        shifted = fixed + (places - fixed + turn * (used - fixed)) % max(1, amount - fixed)
        return jnp.zeros((amount,), jnp.int32).at[sequence[jnp.where(places < fixed, places, shifted)]].set(jnp.asarray(sizes, jnp.int32))

    sizes = jnp.where(number % 4 == 0, named(crowded, number // 4), named(ordinary, number - number // 4 - 1))
    mixed = jax.random.permutation(jax.random.fold_in(own, 3), amount)
    donor, sink = mixed[0:amount // 2 * 2:2], mixed[1:amount // 2 * 2:2]
    margin = jnp.minimum(sizes[donor] - 1, most - sizes[sink]) // 2
    margin = jnp.where((donor == sequence[0]) | (sink == sequence[0]) | (sizes[sink] == 0), 0, jnp.maximum(margin, 0))
    shifted = jax.random.randint(jax.random.fold_in(own, 4), (amount // 2,), 0, 1 << 20) % (margin + 1)
    sizes = sizes.at[donor].add(-shifted).at[sink].add(shifted)
    labels = jnp.searchsorted(jnp.cumsum(sizes), jnp.arange(rows * top), side="right").astype(jnp.int32)
    listing = labels.reshape(top, rows).T
    listing = listing[jax.random.permutation(jax.random.fold_in(own, 1), rows)]
    turn = jax.random.randint(jax.random.fold_in(own, 2), (rows, 1), 0, top)
    return jnp.take_along_axis(listing, (jnp.arange(top)[None, :] + turn) % top, axis=1)


def shares(number_of, total, most, slope, full):
    weights = [(1 << 20) // math.isqrt(rank ** slope) + 1 for rank in range(1, number_of + 1)]
    largest = most if full else min(most, max(-(-total // number_of), total * weights[0] // sum(weights)))
    least = 1 if total - largest >= number_of - 1 else 0
    holding, rest = [largest] + [least] * (number_of - 1), total - largest - least * (number_of - 1)
    while rest > 0:
        candidates = [i for i in range(1, number_of) if holding[i] < largest] or [i for i in range(1, number_of) if holding[i] < most]
        whole, budget = sum([weights[i] for i in candidates]), rest
        for i in candidates:
            extra = min(most - holding[i], max(1, budget * weights[i] // whole), rest)
            holding[i] = holding[i] + extra
            rest = rest - extra
    return np.array(holding)


def bell_draw(stream_key, dims, scale, bound, shards=(), kind=jnp.bfloat16):
    values = scale * jax.random.normal(stream_key, dims, jnp.float32)
    if shards:
        values = values * steps_of(stream_key, dims, shards, -0.22, 0.18)
    return jnp.clip(values, -bound, bound).astype(kind)


def setup_inputs(seed: int = 0) -> dict:
    seeds = jax.random.split(jax.random.key(seed), 10)
    hidden_in = bell_draw(seeds[0], (ROWS, D), 1.0, 6.0, ((0, 128),))
    expert_ids_keys = jax.random.split(jax.random.fold_in(seeds[1], 1), ROWS // MB_ROWS)
    expert_ids_turns = jax.random.permutation(jax.random.fold_in(seeds[1], 3), ROWS // MB_ROWS)
    expert_ids = jax.vmap(lambda own, number: routed_block(jax.random.fold_in(seeds[1], 2), own, number, MB_ROWS, EXPERTS, TOP, CAP, 2))(expert_ids_keys, expert_ids_turns).reshape((ROWS, TOP))
    gate_coef = jnp.clip(0.1 + 0.9 * jax.random.uniform(seeds[2], (ROWS, TOP), jnp.float32) ** steps_of(seeds[2], (ROWS, TOP), ((0, 128),), -0.2, 0.2), 0.1, 1.0)
    query_lat = draw_query_lat(jax.random.fold_in(seeds[9], 71), 0)
    kv_cache = draw_kv_cache(jax.random.fold_in(seeds[9], 71), 0)
    cache_len = draw_cache_len(jax.random.fold_in(seeds[9], 71), 0)
    gate_weight = bell_draw(seeds[6], (EXPERTS, D, FF), D ** -0.5, 0.0625, ((0, 64), (2, 2)))
    up_weight = bell_draw(seeds[7], (EXPERTS, D, FF), D ** -0.5, 0.0625, ((0, 64), (2, 2)))
    down_weight = bell_draw(seeds[8], (EXPERTS, FF, D), FF ** -0.5, 0.1875, ((0, 64), (1, 2)))
    return dict(hidden_in=hidden_in, expert_ids=expert_ids, gate_coef=gate_coef, query_lat=query_lat, kv_cache=kv_cache, cache_len=cache_len, gate_weight=gate_weight, up_weight=up_weight, down_weight=down_weight)


score_scale = 1.0 / math.sqrt(192.0)

def attend(query_lat, kv_cache, cache_len):
    query_f = query_lat.astype(jnp.float32)
    cache_f = kv_cache.astype(jnp.float32)
    scores = jnp.einsum('rhk,rlk->rhl', query_f, cache_f) * score_scale
    positions = jnp.arange(kv_cache.shape[1], dtype=jnp.int32)
    visible = positions[None, None, :] < cache_len[:, None, None]
    scores = jnp.where(visible, scores, jnp.float32(-1e+30))
    top_score = lax.optimization_barrier(jnp.max(scores, axis=2, keepdims=True))
    exponent = jnp.exp(scores - top_score)
    denominator = lax.optimization_barrier(jnp.sum(exponent, axis=2, keepdims=True))
    weights = (exponent / denominator).astype(jnp.bfloat16)
    output = jnp.einsum('rhl,rlc->rhc', weights.astype(jnp.float32), cache_f[:, :, :LAT])
    return output.astype(jnp.bfloat16)

def reference(hidden_in, expert_ids, gate_coef, query_lat, kv_cache, cache_len, gate_weight, up_weight, down_weight):
    attention = attend(query_lat, kv_cache, cache_len)
    block_count = ROWS // MB_ROWS
    per_block = MB_ROWS * TOP
    block_ids = expert_ids.reshape(block_count, per_block).astype(jnp.int32)
    position_ids = jnp.arange(per_block, dtype=jnp.int32)
    matches = (block_ids[:, :, None] == block_ids[:, None, :]) & (position_ids[None, None, :] < position_ids[None, :, None])
    slot_rank = lax.optimization_barrier(jnp.sum(matches.astype(jnp.int32), axis=2)).astype(jnp.int32)
    per_expert = block_count * CAP
    block_base = jnp.arange(block_count, dtype=jnp.int32)[:, None] * CAP
    target = (block_ids * per_expert + block_base + slot_rank).reshape(-1).astype(jnp.int32)
    owner_rows = (jnp.arange(ROWS * TOP, dtype=jnp.int32) // TOP).astype(jnp.int32)
    table = jnp.full((EXPERTS * per_expert,), ROWS, jnp.int32).at[target].set(owner_rows)
    table = table.reshape(EXPERTS, per_expert)
    padded = jnp.concatenate([hidden_in, jnp.zeros((1, D), jnp.bfloat16)], axis=0)
    half_width = FF // N_SEC

    def one_expert(packed):
        row_index, gate_e, up_e, down_e = packed
        tokens = padded[row_index]
        gate_val = jnp.dot(tokens, gate_e, preferred_element_type=jnp.float32)
        up_val = jnp.dot(tokens, up_e, preferred_element_type=jnp.float32)
        hidden = (jax.nn.silu(gate_val) * up_val).astype(jnp.bfloat16)
        running = jnp.zeros((tokens.shape[0], D), jnp.float32)
        for half_index in range(N_SEC):
            lower = half_index * half_width
            part_out = jnp.dot(hidden[:, lower:lower + half_width], down_e[lower:lower + half_width], preferred_element_type=jnp.float32)
            running = running + part_out.astype(jnp.bfloat16).astype(jnp.float32)
        return running.astype(jnp.bfloat16)
    outputs = lax.map(one_expert, (table, gate_weight, up_weight, down_weight))
    flat_out = outputs.reshape(-1, D)
    picked = flat_out[target].astype(jnp.float32).reshape(ROWS, TOP, D)
    routed_out = lax.optimization_barrier(jnp.sum(picked * gate_coef.astype(jnp.float32)[:, :, None], axis=1)).astype(jnp.bfloat16)
    return (attention, routed_out)
```

```python
import functools
import math

import jax
import jax.numpy as jnp
from jax import lax
from jax.experimental import pallas as pl
from jax.experimental.pallas import tpu as pltpu
from jax.sharding import PartitionSpec as P

LAT = 512
TOP = 8
MESH = pl.DeviceIdType.MESH
SCALE = 1.0 / math.sqrt(192.0)

WIDTHS = (2304, 2560, 2304)
OFFSETS = (0, 2304, 4864)
STEPS = (768, 1280, 768)
HALVES = (1152, 1280, 1152)
ORDERS = ((0, 1, 2), (2, 0, 1), (1, 2, 0))
TABLE = 128
LANES = 256


def iota(shape, dim):
    return lax.broadcasted_iota(jnp.int32, shape, dim)


def dot(a, b):
    return jnp.dot(a, b, preferred_element_type=jnp.float32)


def dot_nt(a, b):
    return lax.dot_general(a, b, (((1,), (1,)), ((), ())), preferred_element_type=jnp.float32)


def kernel(
    len_ref,
    ids_ref,
    coef_ref,
    hidden_ref,
    query_ref,
    cache_ref,
    gate_ref,
    up_ref,
    down_ref,
    att_ref,
    out_ref,
    *scratch,
):
    rows_buf = scratch[0:3]
    slot_buf = scratch[3:6]
    recv_buf = scratch[6:9]
    back_buf = scratch[9:12]
    relay_in = scratch[12:15]
    relay_out = scratch[15:18]
    part_buf = scratch[18:21]
    wide_a = scratch[21:24]
    wide_b = scratch[24:27]
    wide_c = scratch[27:30]
    wide_d = scratch[30:33]
    thin_a = scratch[33:36]
    thin_b = scratch[36:39]
    thin_c = scratch[39:42]
    thin_d = scratch[42:45]
    (gate_buf, up_buf, down_buf, acc, hid, hid_p, q_buf, kv_buf, o_buf) = scratch[45:54]
    send_sem, recv_sem, load_sem, own_sem, q_sem, kv_sem, o_sem = scratch[54:]

    sec = lax.axis_index("sec")
    dev = lax.axis_index("dev")
    core = dev % 2
    pos = (dev // 16, ((dev // 8) % 2) * 2 + sec, (dev // 2) % 4)

    def device(point, which):
        x, y, z = point
        return (y % 2, ((x * 2 + y // 2) * 4 + z) * 2 + which)

    def moved(dim, delta):
        point = list(pos)
        point[dim] = (pos[dim] + delta) % 4
        return tuple(point)

    turn = 1 - 2 * core
    pair = 1 - 2 * (pos[1] % 2)

    loads = [
        pltpu.make_async_copy(gate_ref.at[0], gate_buf, load_sem.at[0]),
        pltpu.make_async_copy(up_ref.at[0], up_buf, load_sem.at[1]),
        pltpu.make_async_copy(down_ref.at[0], down_buf, load_sem.at[2]),
    ]
    own = []
    for p in range(3):
        d1, d2, _ = ORDERS[p]
        own.append(
            pltpu.make_async_copy(
                hidden_ref.at[:, pl.ds(OFFSETS[p], WIDTHS[p])],
                rows_buf[p].at[pos[d1], pos[d2], :, pl.ds(0, WIDTHS[p])],
                own_sem.at[p],
            )
        )
        own[p].start()

    barrier = pltpu.get_barrier_semaphore()
    partners = [device(pos, 1 - core)]
    for dim in range(3):
        for delta in (1, -1):
            for which in range(2):
                partners.append(device(moved(dim, delta), which))
    for partner in partners:
        pl.semaphore_signal(barrier, inc=1, device_id=partner, device_id_type=MESH)

    lane = iota((16, TABLE), 1)
    hit = jnp.zeros((16, TABLE), jnp.float32)
    weight = jnp.zeros((16, TABLE), jnp.float32)
    for k in range(TOP):
        match = ids_ref[:, k : k + 1] == lane // 2
        hit = hit + jnp.where(match, 1.0, 0.0)
        weight = weight + jnp.where(match, coef_ref[:, k : k + 1], 0.0)
    low = (iota((16, 16), 1) < iota((16, 16), 0)) & (iota((16, 16), 1) // 8 == iota((16, 16), 0) // 8)
    rank = dot(jnp.where(low, 1.0, 0.0).astype(jnp.bfloat16), hit.astype(jnp.bfloat16))
    table = jnp.where(rank == (lane % 2).astype(jnp.float32), weight, 0.0).astype(jnp.bfloat16)
    for p in range(3):
        d1, d2, _ = ORDERS[p]
        rows_buf[p][pos[d1], pos[d2], :, pl.ds(WIDTHS[p], TABLE)] = table

    for p in range(3):
        own[p].wait()
    pl.semaphore_wait(barrier, len(partners))

    def remote(src, dst, p, send, recv, target):
        return pltpu.make_async_remote_copy(
            src_ref=src,
            dst_ref=dst,
            send_sem=send_sem.at[p, send],
            recv_sem=recv_sem.at[p, recv],
            device_id=target,
            device_id_type=MESH,
        )

    def arrived(dst, p, recv):
        remote(dst, dst, p, 0, recv, device(pos, 1 - core)).wait_recv()

    def q_copy(step, slot):
        return pltpu.make_async_copy(query_ref.at[pl.ds(step * 2, 2)], q_buf.at[slot], q_sem.at[slot])

    def kv_copy(step, slot):
        return pltpu.make_async_copy(cache_ref.at[pl.ds(step * 2, 2)], kv_buf.at[slot], kv_sem.at[slot])

    def o_copy(step, slot):
        return pltpu.make_async_copy(o_buf.at[slot], att_ref.at[pl.ds(step * 2, 2)], o_sem.at[slot])

    def attend(step, carry):
        slot = step % 2
        q_copy(step, slot).wait()
        kv_copy(step, slot).wait()

        @pl.when(step >= 2)
        def _():
            o_copy(step, slot).wait()

        for i in range(2):
            keys = kv_buf[slot, i]
            scores = dot_nt(q_buf[slot, i], keys) * SCALE
            visible = iota((64, 128), 1) < len_ref[step * 2 + i]
            scores = jnp.where(visible, scores, -1e30)
            exponent = jnp.exp(scores - jnp.max(scores, axis=1, keepdims=True))
            weights = (exponent / jnp.sum(exponent, axis=1, keepdims=True)).astype(jnp.bfloat16)
            o_buf[slot, i] = dot(weights, keys[:, :LAT]).astype(jnp.bfloat16)
        o_copy(step, slot).start()

        @pl.when(step + 2 < 8)
        def _():
            q_copy(step + 2, slot).start()
            kv_copy(step + 2, slot).start()

        return carry

    for step in range(2):
        q_copy(step, step).start()
        kv_copy(step, step).start()

    def ring(p, dim, base, block):
        half = HALVES[p]
        rest = WIDTHS[p] + TABLE - half
        here, up, down = pos[dim], (pos[dim] + 1) % 4, (pos[dim] + 3) % 4
        above, below = device(moved(dim, 1), core), device(moved(dim, -1), core)
        first = [
            remote(block(here), block(here), p, base, base, above),
            remote(block(here), block(here), p, base + 1, base + 1, below),
        ]
        low_part = lambda i: block(i, pl.ds(0, half))
        high_part = lambda i: block(i, pl.ds(half, rest))
        second = [
            remote(low_part(down), low_part(down), p, base + 2, base + 2, above),
            remote(high_part(up), high_part(up), p, base + 3, base + 3, below),
        ]
        far = (pos[dim] + 2) % 4
        waits = [
            lambda: arrived(block(down), p, base),
            lambda: arrived(block(up), p, base + 1),
            lambda: arrived(low_part(far), p, base + 2),
            lambda: arrived(high_part(far), p, base + 3),
        ]
        return first, second, waits

    rings_one, rings_two = [], []
    for p in range(3):
        d1, d2, _ = ORDERS[p]

        def block_one(i, columns=slice(None), p=p, d2=d2):
            return rows_buf[p].at[i, pos[d2], :, columns]

        def block_two(i, columns=slice(None), p=p):
            return rows_buf[p].at[:, i, :, columns]

        rings_one.append(ring(p, d1, 0, block_one))
        rings_two.append(ring(p, d2, 4, block_two))

    def begin(rings):
        for first, _, _ in rings:
            for copy in first:
                copy.start()

    def turn_round(rings):
        for _, second, waits in rings:
            for i in range(2):
                waits[i]()
                second[i].start()

    def finish(rings):
        for _, _, waits in rings:
            waits[2]()
            waits[3]()

    def drain(rings):
        for first, second, _ in rings:
            for copy in first + second:
                copy.wait_send()

    begin(rings_one)
    for load in loads:
        load.start()
    lax.fori_loop(0, 1, attend, 0)
    turn_round(rings_one)
    lax.fori_loop(1, 3, attend, 0)
    finish(rings_one)
    begin(rings_two)
    lax.fori_loop(3, 6, attend, 0)
    turn_round(rings_two)
    lax.fori_loop(6, 8, attend, 0)

    def chooser(p):
        n = iota((512, TABLE), 0)
        other, which, slot = n // 128, (n // 64) % 2, n % 2
        if p == 0:
            expert = ((pos[0] * 2 + pos[1] // 2) * 4 + other) * 2 + which
        elif p == 1:
            expert = ((pos[0] * 2 + other // 2) * 4 + pos[2]) * 2 + which
        else:
            expert = ((other * 2 + pos[1] // 2) * 4 + pos[2]) * 2 + which
        return jnp.where(iota((512, TABLE), 1) == expert * 2 + slot, 1.0, 0.0).astype(jnp.bfloat16)

    def table_of(p):
        return rows_buf[p][:, :, :, pl.ds(WIDTHS[p], TABLE)].reshape(256, TABLE)

    def columns_of(i):
        return pl.ds(pl.multiple_of(i * LANES, LANES), LANES)

    sent = []

    def send(copy):
        copy.start()
        sent.append(copy)

    local = []
    for p in range(3):
        _, _, d3 = ORDERS[p]
        for wait in rings_two[p][2][2:]:
            wait()
        hot = dot_nt(chooser(p), table_of(p))
        near = (iota((512, 256), 0) % 64) // 2 == iota((512, 256), 1) // 8
        picker = jnp.where(near & (hot != 0.0), 1.0, 0.0).astype(jnp.bfloat16)

        def pick(i, carry, p=p, picker=picker):
            block = rows_buf[p][:, :, :, columns_of(i)].reshape(256, LANES)
            slot_buf[p][:, :, columns_of(i)] = dot(picker, block).astype(jnp.bfloat16).reshape(8, 64, LANES)
            return carry

        lax.fori_loop(0, WIDTHS[p] // LANES, pick, 0)

        here = pos[d3]
        far = (here + 2) % 4
        mine = core * 4 + here
        if d3 != 1:
            for delta in (1, -1):
                there = (here + delta) % 4
                for which in range(2):
                    target = device(moved(d3, delta), which)
                    send(remote(slot_buf[p].at[there * 2 + which], recv_buf[p].at[mine], p, 8 + (delta + 1) + which, 8 + mine, target))
            for which, delta in ((0, 1), (1, -1)):
                target = device(moved(d3, delta), which)
                send(remote(slot_buf[p].at[far * 2 + which], relay_in[p].at[core], p, 12 + which, 16 + core, target))
        else:
            for delta, base in ((-pair, 8), (pair, 10)):
                there = (here + delta) % 4
                for which in range(2):
                    target = device(moved(d3, delta), which)
                    send(remote(slot_buf[p].at[there * 2 + which], recv_buf[p].at[mine], p, base + which, 8 + mine, target))
        send(remote(slot_buf[p].at[here * 2 + 1 - core], recv_buf[p].at[mine], p, 14, 8 + mine, device(pos, 1 - core)))
        local.append(pltpu.make_async_copy(slot_buf[p].at[here * 2 + core], recv_buf[p].at[mine], own_sem.at[3 + p]))
        local[p].start()

    for p in range(3):
        _, _, d3 = ORDERS[p]
        here = pos[d3]
        for c in range(2):
            if d3 != 1:
                arrived(relay_in[p].at[c], p, 16 + c)
                source = (here - turn) % 4
                entry = c * 4 + source
                send(remote(relay_in[p].at[c], recv_buf[p].at[entry], p, 18 + c, 8 + entry, device(moved(d3, turn), core)))
            else:
                source = (here - pair) % 4
                entry = c * 4 + source
                arrived(recv_buf[p].at[entry], p, 8 + entry)
                send(remote(recv_buf[p].at[entry], recv_buf[p].at[entry], p, 18 + c, 8 + entry, device(moved(d3, pair), core)))

    for p in range(3):
        _, _, d3 = ORDERS[p]
        here = pos[d3]
        for c in range(2):
            for delta in (1, 3, 2):
                entry = c * 4 + (here + delta) % 4
                if d3 != 1:
                    arrived(recv_buf[p].at[entry], p, 8 + entry)
        if d3 == 1:
            for c in range(2):
                for delta in (pair, 2):
                    entry = c * 4 + (here + delta) % 4
                    arrived(recv_buf[p].at[entry], p, 8 + entry)
        arrived(recv_buf[p].at[(1 - core) * 4 + here], p, 8 + (1 - core) * 4 + here)
        local[p].wait()
    for copy in sent:
        copy.wait_send()
    drain(rings_one)
    drain(rings_two)
    for step in (6, 7):
        o_copy(step, step % 2).wait()
    for load in loads:
        load.wait()

    def source_row(p, i):
        z, x, y, q = i // 64, (i // 16) % 4, (i // 4) % 4, i % 4
        if p == 1:
            return y * 64 + z * 16 + x * 4 + q
        return x * 64 + y * 16 + z * 4 + q

    acc[...] = jnp.zeros_like(acc)
    for p in range(3):
        held = recv_buf[p]
        if p > 0:
            held = slot_buf[p]
            order = jnp.where(source_row(p, iota((256, 256), 0)) == iota((256, 256), 1), 1.0, 0.0).astype(jnp.bfloat16)

            def straighten(i, carry, p=p, order=order):
                for c in range(2):
                    block = recv_buf[p][pl.ds(c * 4, 4), :, columns_of(i)].reshape(256, LANES)
                    slot_buf[p][pl.ds(c * 4, 4), :, columns_of(i)] = dot(order, block).astype(jnp.bfloat16).reshape(4, 64, LANES)
                return carry

            lax.fori_loop(0, WIDTHS[p] // LANES, straighten, 0)

        def widen(i, carry, p=p, held=held):
            step = STEPS[p]
            start = pl.multiple_of(i * step, 256)
            block = held[:, :, pl.ds(start, step)].reshape(512, step)
            deep = pl.ds(pl.multiple_of(OFFSETS[p] + start, 256), step)
            for n in range(2):
                acc[:, n * 256 : n * 256 + 256] += dot(block, gate_buf[deep, n * 256 : n * 256 + 256])
                acc[:, 512 + n * 256 : 768 + n * 256] += dot(block, up_buf[deep, n * 256 : n * 256 + 256])
            return carry

        lax.fori_loop(0, WIDTHS[p] // STEPS[p], widen, 0)

    def activate(i, carry):
        rows = pl.ds(pl.multiple_of(i * 64, 64), 64)
        gate_val = acc[rows, 0:512]
        hid[rows, :] = ((gate_val / (1.0 + jnp.exp(-gate_val))) * acc[rows, 512:1024]).astype(jnp.bfloat16)
        return carry

    lax.fori_loop(0, 8, activate, 0)

    returned = []

    def give(copy):
        copy.start()
        returned.append(copy)

    for p in range(3):
        _, _, d3 = ORDERS[p]
        if p == 0:
            hid_p[...] = hid[...]
        else:
            order = jnp.where(source_row(p, iota((256, 256), 1)) == iota((256, 256), 0), 1.0, 0.0).astype(jnp.bfloat16)
            for c in range(2):
                hid_p[c * 256 : c * 256 + 256, :] = dot(order, hid[c * 256 : c * 256 + 256, :]).astype(jnp.bfloat16)

        def narrow(i, carry, p=p):
            deep = pl.ds(pl.multiple_of(OFFSETS[p] + i * LANES, LANES), LANES)
            recv_buf[p][:, :, columns_of(i)] = dot(hid_p[...], down_buf[:, deep]).astype(jnp.bfloat16).reshape(8, 64, LANES)
            return carry

        lax.fori_loop(0, WIDTHS[p] // LANES, narrow, 0)

        here = pos[d3]
        far = (here + 2) % 4
        entry = here * 2 + core
        for delta, base in ((1, 20), (-1, 22)):
            there = (here + delta) % 4
            for c in range(2):
                give(remote(recv_buf[p].at[c * 4 + there], back_buf[p].at[entry], p, base + c, 20 + entry, device(moved(d3, delta), c)))
        step = turn if d3 != 1 else pair
        for c in range(2):
            give(remote(recv_buf[p].at[c * 4 + far], relay_out[p].at[c], p, 24 + c, 28 + c, device(moved(d3, step), core)))
        give(remote(recv_buf[p].at[(1 - core) * 4 + here], back_buf[p].at[entry], p, 26, 20 + entry, device(pos, 1 - core)))
        local[p] = pltpu.make_async_copy(recv_buf[p].at[core * 4 + here], back_buf[p].at[entry], own_sem.at[6 + p])
        local[p].start()

    for p in range(3):
        _, _, d3 = ORDERS[p]
        here = pos[d3]
        step = turn if d3 != 1 else -pair
        origin = -turn if d3 != 1 else pair
        entry = ((here + origin) % 4) * 2 + core
        for c in range(2):
            arrived(relay_out[p].at[c], p, 28 + c)
            give(remote(relay_out[p].at[c], back_buf[p].at[entry], p, 28 + c, 20 + entry, device(moved(d3, step), c)))

    def fold(p, dim, base, block, bufs):
        half = HALVES[p]
        rest = WIDTHS[p] - half
        here, up, down, far = pos[dim], (pos[dim] + 1) % 4, (pos[dim] + 3) % 4, (pos[dim] + 2) % 4
        above, below = device(moved(dim, 1), core), device(moved(dim, -1), core)
        low_part = lambda i: block(i, pl.ds(0, half))
        high_part = lambda i: block(i, pl.ds(half, rest))
        first = [
            remote(low_part(far), bufs[0], p, base, base, above),
            remote(high_part(far), bufs[1], p, base + 1, base + 1, below),
        ]
        second = [
            remote(block(up), bufs[2], p, base + 2, base + 2, above),
            remote(block(down), bufs[3], p, base + 3, base + 3, below),
        ]
        return first, second, low_part(up), high_part(down)

    folds_two, folds_one = [], []
    for p in range(3):
        d1, d2, d3 = ORDERS[p]
        here = pos[d3]
        arrivals = [(here * 2 + 1 - core)]
        for delta in (1, 2, 3):
            for which in range(2):
                arrivals.append(((here + delta) % 4) * 2 + which)
        for entry in arrivals:
            arrived(back_buf[p].at[entry], p, 20 + entry)
        local[p].wait()
        near = (iota((256, 512), 1) % 64) // 2 == iota((256, 512), 0) // 8
        mixer = jnp.where(near, dot_nt(table_of(p), chooser(p)), 0.0).astype(jnp.bfloat16)

        def mix(i, carry, p=p, mixer=mixer):
            block = back_buf[p][:, :, columns_of(i)].reshape(512, LANES)
            part_buf[p][:, :, :, columns_of(i)] = dot(mixer, block).astype(jnp.bfloat16).reshape(4, 4, 16, LANES)
            return carry

        lax.fori_loop(0, WIDTHS[p] // LANES, mix, 0)

        def block_two(i, columns=slice(None), p=p):
            return part_buf[p].at[:, i, :, columns]

        def block_one(i, columns=slice(None), p=p, d2=d2):
            return part_buf[p].at[i, pos[d2], :, columns]

        folds_two.append(fold(p, d2, 30, block_two, (wide_a[p], wide_b[p], wide_c[p], wide_d[p])))
        folds_one.append(fold(p, d1, 34, block_one, (thin_a[p], thin_b[p], thin_c[p], thin_d[p])))
        for copy in folds_two[p][0]:
            give(copy)

    def add_into(ref, *others):
        total = ref[...].astype(jnp.float32)
        for other in others:
            total = total + other[...].astype(jnp.float32)
        ref[...] = total.astype(jnp.bfloat16)

    for p in range(3):
        first, second, low_up, high_down = folds_two[p]
        arrived(wide_a[p], p, 30)
        add_into(low_up, wide_a[p])
        give(second[0])
        arrived(wide_b[p], p, 31)
        add_into(high_down, wide_b[p])
        give(second[1])
    for p in range(3):
        d1, d2, d3 = ORDERS[p]
        arrived(wide_c[p], p, 32)
        arrived(wide_d[p], p, 33)
        add_into(part_buf[p].at[:, pos[d2]], wide_c[p], wide_d[p])
        for copy in folds_one[p][0]:
            give(copy)
    for p in range(3):
        first, second, low_up, high_down = folds_one[p]
        arrived(thin_a[p], p, 34)
        add_into(low_up, thin_a[p])
        give(second[0])
        arrived(thin_b[p], p, 35)
        add_into(high_down, thin_b[p])
        give(second[1])
    for p in range(3):
        d1, d2, d3 = ORDERS[p]
        arrived(thin_c[p], p, 36)
        arrived(thin_d[p], p, 37)
        total = part_buf[p][pos[d1], pos[d2]].astype(jnp.float32)
        total = total + thin_c[p][...].astype(jnp.float32) + thin_d[p][...].astype(jnp.float32)
        out_ref[:, pl.ds(OFFSETS[p], WIDTHS[p])] = total.astype(jnp.bfloat16)
    for copy in returned:
        copy.wait_send()


def per_device(
    hidden_in,
    expert_ids,
    gate_coef,
    query_lat,
    kv_cache,
    cache_len,
    gate_weight,
    up_weight,
    down_weight,
):
    bf16, f32 = jnp.bfloat16, jnp.float32
    vmem = lambda *shape, dtype=bf16: pltpu.VMEM(shape, dtype)
    dma = pltpu.SemaphoreType.DMA
    scratch = (
        [vmem(4, 4, 16, w + TABLE) for w in WIDTHS]
        + [vmem(8, 64, w) for w in WIDTHS]
        + [vmem(8, 64, w) for w in WIDTHS]
        + [vmem(8, 64, w) for w in WIDTHS]
        + [vmem(2, 64, w) if i != 1 else vmem(2, 64, 128) for i, w in enumerate(WIDTHS)]
        + [vmem(2, 64, w) for w in WIDTHS]
        + [vmem(4, 4, 16, w) for w in WIDTHS]
        + [vmem(4, 16, h) for h in HALVES]
        + [vmem(4, 16, w - h) for w, h in zip(WIDTHS, HALVES)]
        + [vmem(4, 16, w) for w in WIDTHS]
        + [vmem(4, 16, w) for w in WIDTHS]
        + [vmem(16, h) for h in HALVES]
        + [vmem(16, w - h) for w, h in zip(WIDTHS, HALVES)]
        + [vmem(16, w) for w in WIDTHS]
        + [vmem(16, w) for w in WIDTHS]
        + [
            vmem(7168, 512),
            vmem(7168, 512),
            vmem(512, 7168),
            vmem(512, 1024, dtype=f32),
            vmem(512, 512),
            vmem(512, 512),
            vmem(2, 2, 64, 576),
            vmem(2, 2, 128, 576),
            vmem(2, 2, 64, 512),
            dma((3, 38)),
            dma((3, 38)),
            dma((3,)),
            dma((9,)),
            dma((2,)),
            dma((2,)),
            dma((2,)),
        ]
    )
    anywhere = pl.BlockSpec(memory_space=pl.ANY)
    in_vmem = pl.BlockSpec(memory_space=pltpu.VMEM)
    return pl.pallas_call(
        kernel,
        out_shape=(
            jax.ShapeDtypeStruct((16, 64, 512), bf16),
            jax.ShapeDtypeStruct((16, 7168), bf16),
        ),
        in_specs=[pl.BlockSpec(memory_space=pltpu.SMEM), in_vmem, in_vmem] + [anywhere] * 6,
        out_specs=(anywhere, in_vmem),
        scratch_shapes=scratch,
        compiler_params=pltpu.CompilerParams(
            collective_id=0, has_side_effects=True, vmem_limit_bytes=67043328
        ),
        name="moe_step",
    )(
        cache_len,
        expert_ids,
        gate_coef,
        hidden_in,
        query_lat,
        kv_cache,
        gate_weight,
        up_weight,
        down_weight,
    )


def solution(mesh):
    in_specs = (
        P(("sec", "dev"), None),
        P(("sec", "dev"), None),
        P(("sec", "dev"), None),
        P(("sec", "dev"), None, None),
        P(("sec", "dev"), None, None),
        P(("sec", "dev")),
        P("dev", None, "sec"),
        P("dev", None, "sec"),
        P("dev", "sec", None),
    )
    out_specs = (P(("sec", "dev"), None, None), P(("sec", "dev"), None))
    return jax.shard_map(
        per_device, mesh=mesh, in_specs=in_specs, out_specs=out_specs, check_vma=False
    )
```

```python
import functools
import math

import jax
import jax.numpy as jnp
from jax import lax
from jax.experimental import pallas as pl
from jax.experimental.pallas import tpu as pltpu
from jax.sharding import PartitionSpec as P

LAT = 512
TOP = 8
MESH = pl.DeviceIdType.MESH
SCALE = 1.0 / math.sqrt(192.0)

WIDTHS = (1280, 1280, 1024, 1024, 1280, 1280)
OFFSETS = (0, 1280, 2560, 3584, 4608, 5888)
EXTRA = (128, 128, 128, 0, 0, 0)
ORDERS = ((0, 1, 2), (2, 0, 1), (1, 2, 0)) * 2
PIECES = 6
GROUP_A, GROUP_B = (0, 1, 2), (3, 4, 5)
TABLE = 128
LANES = 256


def iota(shape, dim):
    return lax.broadcasted_iota(jnp.int32, shape, dim)


def dot(a, b):
    return jnp.dot(a, b, preferred_element_type=jnp.float32)


def dot_nt(a, b):
    return lax.dot_general(a, b, (((1,), (1,)), ((), ())), preferred_element_type=jnp.float32)


def kernel(
    len_ref,
    ids_ref,
    coef_ref,
    hidden_ref,
    query_ref,
    cache_ref,
    gate_ref,
    up_ref,
    down_ref,
    att_ref,
    out_ref,
    *scratch,
):
    many = [scratch[i * PIECES : (i + 1) * PIECES] for i in range(15)]
    rows_buf, slot_buf, recv_buf, back_buf, relay_in, relay_out, part_buf = many[:7]
    wide_a, wide_b, wide_c, wide_d, thin_a, thin_b, thin_c, thin_d = many[7:]
    (gate_buf, up_buf, down_buf, acc, hid, hid_p, q_buf, kv_buf, o_buf) = scratch[90:99]
    send_sem, recv_sem, load_sem, own_sem, q_sem, kv_sem, o_sem = scratch[99:]

    sec = lax.axis_index("sec")
    dev = lax.axis_index("dev")
    core = dev % 2
    pos = (dev // 16, ((dev // 8) % 2) * 2 + sec, (dev // 2) % 4)

    def device(point, which):
        x, y, z = point
        return (y % 2, ((x * 2 + y // 2) * 4 + z) * 2 + which)

    def moved(dim, delta):
        point = list(pos)
        point[dim] = (pos[dim] + delta) % 4
        return tuple(point)

    turn = 1 - 2 * core
    pair = 1 - 2 * (pos[1] % 2)

    loads = [
        pltpu.make_async_copy(gate_ref.at[0], gate_buf, load_sem.at[0]),
        pltpu.make_async_copy(up_ref.at[0], up_buf, load_sem.at[1]),
        pltpu.make_async_copy(down_ref.at[0], down_buf, load_sem.at[2]),
    ]
    own = []
    for p in range(PIECES):
        d1, d2, _ = ORDERS[p]
        own.append(
            pltpu.make_async_copy(
                hidden_ref.at[:, pl.ds(OFFSETS[p], WIDTHS[p])],
                rows_buf[p].at[pos[d1], pos[d2], :, pl.ds(0, WIDTHS[p])],
                own_sem.at[p],
            )
        )
        own[p].start()

    barrier = pltpu.get_barrier_semaphore()
    partners = [device(pos, 1 - core)]
    for dim in range(3):
        for delta in (1, -1):
            for which in range(2):
                partners.append(device(moved(dim, delta), which))
    for partner in partners:
        pl.semaphore_signal(barrier, inc=1, device_id=partner, device_id_type=MESH)

    eye = jnp.where(iota((16, 16), 0) == iota((16, 16), 1), 1.0, 0.0).astype(jnp.bfloat16)
    names = dot_nt(eye, ids_ref[...].astype(jnp.float32).astype(jnp.bfloat16))
    coefs = dot_nt(eye, coef_ref[...].astype(jnp.bfloat16))
    lane = iota((16, TABLE), 1)
    expert_of = (lane // 2).astype(jnp.float32)
    hit = jnp.zeros((16, TABLE), jnp.float32)
    weight = jnp.zeros((16, TABLE), jnp.float32)
    for k in range(TOP):
        match = names[:, k : k + 1] == expert_of
        hit = hit + jnp.where(match, 1.0, 0.0)
        weight = weight + jnp.where(match, coefs[:, k : k + 1], 0.0)
    low = (iota((16, 16), 1) < iota((16, 16), 0)) & (iota((16, 16), 1) // 8 == iota((16, 16), 0) // 8)
    rank = dot(jnp.where(low, 1.0, 0.0).astype(jnp.bfloat16), hit.astype(jnp.bfloat16))
    table = jnp.where(rank == (lane % 2).astype(jnp.float32), weight, 0.0).astype(jnp.bfloat16)
    for p in GROUP_A:
        d1, d2, _ = ORDERS[p]
        rows_buf[p][pos[d1], pos[d2], :, pl.ds(WIDTHS[p], TABLE)] = table

    for p in range(PIECES):
        own[p].wait()
    pl.semaphore_wait(barrier, len(partners))

    def remote(src, dst, p, send, recv, target):
        return pltpu.make_async_remote_copy(
            src_ref=src,
            dst_ref=dst,
            send_sem=send_sem.at[p, send],
            recv_sem=recv_sem.at[p, recv],
            device_id=target,
            device_id_type=MESH,
        )

    def arrived(dst, p, recv):
        remote(dst, dst, p, 0, recv, device(pos, 1 - core)).wait_recv()

    def q_copy(step, slot):
        return pltpu.make_async_copy(query_ref.at[pl.ds(step * 2, 2)], q_buf.at[slot], q_sem.at[slot])

    def kv_copy(step, slot):
        return pltpu.make_async_copy(cache_ref.at[pl.ds(step * 2, 2)], kv_buf.at[slot], kv_sem.at[slot])

    def o_copy(step, slot):
        return pltpu.make_async_copy(o_buf.at[slot], att_ref.at[pl.ds(step * 2, 2)], o_sem.at[slot])

    def attend(step, carry):
        slot = step % 2
        q_copy(step, slot).wait()
        kv_copy(step, slot).wait()

        @pl.when(step >= 2)
        def _():
            o_copy(step, slot).wait()

        for i in range(2):
            keys = kv_buf[slot, i]
            scores = dot(q_buf[slot, i], keys) * SCALE
            visible = iota((64, 128), 1) < len_ref[step * 2 + i]
            scores = jnp.where(visible, scores, -1e30)
            exponent = jnp.exp(scores - jnp.max(scores, axis=1, keepdims=True))
            weights = (exponent / jnp.sum(exponent, axis=1, keepdims=True)).astype(jnp.bfloat16)
            o_buf[slot, i] = dot_nt(weights, keys[:LAT, :]).astype(jnp.bfloat16)
        o_copy(step, slot).start()

        @pl.when(step + 2 < 8)
        def _():
            q_copy(step + 2, slot).start()
            kv_copy(step + 2, slot).start()

        return carry

    for step in range(2):
        q_copy(step, step).start()
        kv_copy(step, step).start()

    def ring(p, dim, base, block):
        half = WIDTHS[p] // 2
        rest = half + EXTRA[p]
        here, up, down = pos[dim], (pos[dim] + 1) % 4, (pos[dim] + 3) % 4
        above, below = device(moved(dim, 1), core), device(moved(dim, -1), core)
        first = [
            remote(block(here), block(here), p, base, base, above),
            remote(block(here), block(here), p, base + 1, base + 1, below),
        ]
        low_part = lambda i: block(i, pl.ds(0, half))
        high_part = lambda i: block(i, pl.ds(half, rest))
        second = [
            remote(low_part(down), low_part(down), p, base + 2, base + 2, above),
            remote(high_part(up), high_part(up), p, base + 3, base + 3, below),
        ]
        far = (pos[dim] + 2) % 4
        waits = [
            lambda: arrived(block(down), p, base),
            lambda: arrived(block(up), p, base + 1),
            lambda: arrived(low_part(far), p, base + 2),
            lambda: arrived(high_part(far), p, base + 3),
        ]
        return first, second, waits

    rings_one, rings_two = [], []
    for p in range(PIECES):
        d1, d2, _ = ORDERS[p]

        def block_one(i, columns=slice(None), p=p, d2=d2):
            return rows_buf[p].at[i, pos[d2], :, columns]

        def block_two(i, columns=slice(None), p=p):
            return rows_buf[p].at[:, i, :, columns]

        rings_one.append(ring(p, d1, 0, block_one))
        rings_two.append(ring(p, d2, 4, block_two))

    def begin(rings, group):
        for p in group:
            for copy in rings[p][0]:
                copy.start()

    def turn_round(rings, group):
        for p in group:
            _, second, waits = rings[p]
            for i in range(2):
                waits[i]()
                second[i].start()

    def finish(rings, p):
        waits = rings[p][2]
        waits[2]()
        waits[3]()

    def drain(rings):
        for first, second, _ in rings:
            for copy in first + second:
                copy.wait_send()

    def chooser(p):
        n = iota((512, TABLE), 0)
        other, which, slot = n // 128, (n // 64) % 2, n % 2
        if ORDERS[p][2] == 2:
            expert = ((pos[0] * 2 + pos[1] // 2) * 4 + other) * 2 + which
        elif ORDERS[p][2] == 1:
            expert = ((pos[0] * 2 + other // 2) * 4 + pos[2]) * 2 + which
        else:
            expert = ((other * 2 + pos[1] // 2) * 4 + pos[2]) * 2 + which
        return jnp.where(iota((512, TABLE), 1) == expert * 2 + slot, 1.0, 0.0).astype(jnp.bfloat16)

    def table_of(p):
        first = p % 3
        return rows_buf[first][:, :, :, pl.ds(WIDTHS[first], TABLE)].reshape(256, TABLE)

    def columns_of(i):
        return pl.ds(pl.multiple_of(i * LANES, LANES), LANES)

    sent = [[] for _ in range(PIECES)]
    local = [None] * PIECES

    def spread(p):
        _, _, d3 = ORDERS[p]
        finish(rings_two, p)
        hot = dot_nt(chooser(p), table_of(p))
        near = (iota((512, 256), 0) % 64) // 2 == iota((512, 256), 1) // 8
        picker = jnp.where(near & (hot != 0.0), 1.0, 0.0).astype(jnp.bfloat16)

        def pick(i, carry):
            block = rows_buf[p][:, :, :, columns_of(i)].reshape(256, LANES)
            slot_buf[p][:, :, columns_of(i)] = dot(picker, block).astype(jnp.bfloat16).reshape(8, 64, LANES)
            return carry

        lax.fori_loop(0, WIDTHS[p] // LANES, pick, 0)

        def send(copy):
            copy.start()
            sent[p].append(copy)

        here = pos[d3]
        far = (here + 2) % 4
        mine = core * 4 + here
        if d3 != 1:
            for which, delta in ((0, 1), (1, -1)):
                target = device(moved(d3, delta), which)
                send(remote(slot_buf[p].at[far * 2 + which], relay_in[p].at[core], p, 12 + which, 16 + core, target))
            deltas = ((1, 10), (-1, 8))
        else:
            deltas = ((-pair, 8), (pair, 10))
        for delta, base in deltas:
            there = (here + delta) % 4
            for which in range(2):
                target = device(moved(d3, delta), which)
                send(remote(slot_buf[p].at[there * 2 + which], recv_buf[p].at[mine], p, base + which, 8 + mine, target))
        send(remote(slot_buf[p].at[here * 2 + 1 - core], recv_buf[p].at[mine], p, 14, 8 + mine, device(pos, 1 - core)))
        local[p] = pltpu.make_async_copy(slot_buf[p].at[here * 2 + core], recv_buf[p].at[mine], own_sem.at[PIECES + p])
        local[p].start()

    def relay(p):
        _, _, d3 = ORDERS[p]
        here = pos[d3]
        for c in range(2):
            if d3 != 1:
                arrived(relay_in[p].at[c], p, 16 + c)
                entry = c * 4 + (here - turn) % 4
                copy = remote(relay_in[p].at[c], recv_buf[p].at[entry], p, 18 + c, 8 + entry, device(moved(d3, turn), core))
            else:
                entry = c * 4 + (here - pair) % 4
                arrived(recv_buf[p].at[entry], p, 8 + entry)
                copy = remote(recv_buf[p].at[entry], recv_buf[p].at[entry], p, 18 + c, 8 + entry, device(moved(d3, pair), core))
            copy.start()
            sent[p].append(copy)

    def collect(p):
        _, _, d3 = ORDERS[p]
        here = pos[d3]
        for c in range(2):
            for delta in (1, 3, 2) if d3 != 1 else (pair, 2):
                entry = c * 4 + (here + delta) % 4
                arrived(recv_buf[p].at[entry], p, 8 + entry)
        entry = (1 - core) * 4 + here
        arrived(recv_buf[p].at[entry], p, 8 + entry)
        local[p].wait()
        for copy in sent[p]:
            copy.wait_send()

    def source_row(p, i):
        z, x, y, q = i // 64, (i // 16) % 4, (i // 4) % 4, i % 4
        if ORDERS[p][2] == 1:
            return y * 64 + z * 16 + x * 4 + q
        return x * 64 + y * 16 + z * 4 + q

    def widen(p):
        held = recv_buf[p]
        if ORDERS[p][2] != 2:
            held = slot_buf[p]
            order = jnp.where(source_row(p, iota((256, 256), 0)) == iota((256, 256), 1), 1.0, 0.0).astype(jnp.bfloat16)

            def straighten(i, carry):
                for c in range(2):
                    block = recv_buf[p][pl.ds(c * 4, 4), :, columns_of(i)].reshape(256, LANES)
                    slot_buf[p][pl.ds(c * 4, 4), :, columns_of(i)] = dot(order, block).astype(jnp.bfloat16).reshape(4, 64, LANES)
                return carry

            lax.fori_loop(0, WIDTHS[p] // LANES, straighten, 0)
        block = held[...].reshape(512, WIDTHS[p])
        deep = slice(OFFSETS[p], OFFSETS[p] + WIDTHS[p])
        for n in range(2):
            for base, buf in ((0, gate_buf), (512, up_buf)):
                product = dot(block, buf[deep, n * 256 : n * 256 + 256])
                columns = slice(base + n * 256, base + n * 256 + 256)
                if p == 0:
                    acc[:, columns] = product
                else:
                    acc[:, columns] += product

    def activate(i, carry):
        rows = pl.ds(pl.multiple_of(i * 64, 64), 64)
        gate_val = acc[rows, 0:512]
        hid[rows, :] = ((gate_val / (1.0 + jnp.exp(-gate_val))) * acc[rows, 512:1024]).astype(jnp.bfloat16)
        return carry

    begin(rings_one, GROUP_A)
    begin(rings_one, GROUP_B)
    for load in loads:
        load.start()
    lax.fori_loop(0, 1, attend, 0)
    turn_round(rings_one, GROUP_A)
    turn_round(rings_one, GROUP_B)
    lax.fori_loop(1, 2, attend, 0)
    for p in GROUP_A + GROUP_B:
        finish(rings_one, p)
        begin(rings_two, (p,))
    lax.fori_loop(2, 5, attend, 0)
    turn_round(rings_two, GROUP_A)
    lax.fori_loop(5, 7, attend, 0)
    for p in GROUP_A:
        spread(p)
    turn_round(rings_two, GROUP_B)
    lax.fori_loop(7, 8, attend, 0)
    for p in GROUP_A:
        relay(p)
    for p in GROUP_B:
        spread(p)
    loads[0].wait()
    loads[1].wait()
    for p in GROUP_A:
        collect(p)
        widen(p)
        relay(p + 3)
    for p in GROUP_B:
        collect(p)
        widen(p)
    drain(rings_one)
    drain(rings_two)
    for step in (6, 7):
        o_copy(step, step % 2).wait()
    loads[2].wait()
    lax.fori_loop(0, 8, activate, 0)

    returned = []

    def give(copy):
        copy.start()
        returned.append(copy)

    def narrow(p):
        _, _, d3 = ORDERS[p]
        if d3 == 2:
            hid_p[...] = hid[...]
        else:
            order = jnp.where(source_row(p, iota((256, 256), 1)) == iota((256, 256), 0), 1.0, 0.0).astype(jnp.bfloat16)
            for c in range(2):
                hid_p[c * 256 : c * 256 + 256, :] = dot(order, hid[c * 256 : c * 256 + 256, :]).astype(jnp.bfloat16)

        def shrink(i, carry):
            deep = pl.ds(pl.multiple_of(OFFSETS[p] + i * LANES, LANES), LANES)
            recv_buf[p][:, :, columns_of(i)] = dot(hid_p[...], down_buf[:, deep]).astype(jnp.bfloat16).reshape(8, 64, LANES)
            return carry

        lax.fori_loop(0, WIDTHS[p] // LANES, shrink, 0)

        here = pos[d3]
        far = (here + 2) % 4
        entry = here * 2 + core
        step = turn if d3 != 1 else pair
        for c in range(2):
            give(remote(recv_buf[p].at[c * 4 + far], relay_out[p].at[c], p, 24 + c, 28 + c, device(moved(d3, step), core)))
        for delta, base in ((1, 20), (-1, 22)):
            there = (here + delta) % 4
            for c in range(2):
                give(remote(recv_buf[p].at[c * 4 + there], back_buf[p].at[entry], p, base + c, 20 + entry, device(moved(d3, delta), c)))
        give(remote(recv_buf[p].at[(1 - core) * 4 + here], back_buf[p].at[entry], p, 26, 20 + entry, device(pos, 1 - core)))
        local[p] = pltpu.make_async_copy(recv_buf[p].at[core * 4 + here], back_buf[p].at[entry], own_sem.at[2 * PIECES + p])
        local[p].start()

    def relay_back(p):
        _, _, d3 = ORDERS[p]
        here = pos[d3]
        step = turn if d3 != 1 else -pair
        origin = -turn if d3 != 1 else pair
        entry = ((here + origin) % 4) * 2 + core
        for c in range(2):
            arrived(relay_out[p].at[c], p, 28 + c)
            give(remote(relay_out[p].at[c], back_buf[p].at[entry], p, 28 + c, 20 + entry, device(moved(d3, step), c)))

    def fold(p, dim, base, block, bufs):
        half = WIDTHS[p] // 2
        rest = half
        here, up, down, far = pos[dim], (pos[dim] + 1) % 4, (pos[dim] + 3) % 4, (pos[dim] + 2) % 4
        above, below = device(moved(dim, 1), core), device(moved(dim, -1), core)
        low_part = lambda i: block(i, pl.ds(0, half))
        high_part = lambda i: block(i, pl.ds(half, rest))
        first = [
            remote(low_part(far), bufs[0], p, base, base, above),
            remote(high_part(far), bufs[1], p, base + 1, base + 1, below),
        ]
        second = [
            remote(block(up), bufs[2], p, base + 2, base + 2, above),
            remote(block(down), bufs[3], p, base + 3, base + 3, below),
        ]
        return first, second, low_part(up), high_part(down)

    folds_two, folds_one = [None] * PIECES, [None] * PIECES

    def merge(p):
        d1, d2, d3 = ORDERS[p]
        here = pos[d3]
        arrivals = [(here * 2 + 1 - core)]
        for delta in (1, 2, 3):
            for which in range(2):
                arrivals.append(((here + delta) % 4) * 2 + which)
        for entry in arrivals:
            arrived(back_buf[p].at[entry], p, 20 + entry)
        local[p].wait()
        near = (iota((256, 512), 1) % 64) // 2 == iota((256, 512), 0) // 8
        mixer = jnp.where(near, dot_nt(table_of(p), chooser(p)), 0.0).astype(jnp.bfloat16)

        def mix(i, carry):
            block = back_buf[p][:, :, columns_of(i)].reshape(512, LANES)
            part_buf[p][:, :, :, columns_of(i)] = dot(mixer, block).astype(jnp.bfloat16).reshape(4, 4, 16, LANES)
            return carry

        lax.fori_loop(0, WIDTHS[p] // LANES, mix, 0)
        block_two = lambda i, columns=slice(None): part_buf[p].at[:, i, :, columns]
        block_one = lambda i, columns=slice(None): part_buf[p].at[i, pos[d2], :, columns]
        folds_two[p] = fold(p, d2, 30, block_two, (wide_a[p], wide_b[p], wide_c[p], wide_d[p]))
        folds_one[p] = fold(p, d1, 34, block_one, (thin_a[p], thin_b[p], thin_c[p], thin_d[p]))
        for copy in folds_two[p][0]:
            give(copy)

    def add_into(ref, *others):
        total = ref[...].astype(jnp.float32)
        for other in others:
            total = total + other[...].astype(jnp.float32)
        ref[...] = total.astype(jnp.bfloat16)

    def halfway(p, folds, base, low_buf, high_buf):
        _, second, low_up, high_down = folds[p]
        arrived(low_buf[p], p, base)
        add_into(low_up, low_buf[p])
        give(second[0])
        arrived(high_buf[p], p, base + 1)
        add_into(high_down, high_buf[p])
        give(second[1])

    def close_two(p):
        arrived(wide_c[p], p, 32)
        arrived(wide_d[p], p, 33)
        add_into(part_buf[p].at[:, pos[ORDERS[p][1]]], wide_c[p], wide_d[p])
        for copy in folds_one[p][0]:
            give(copy)

    def close_one(p):
        d1, d2, _ = ORDERS[p]
        arrived(thin_c[p], p, 36)
        arrived(thin_d[p], p, 37)
        total = part_buf[p][pos[d1], pos[d2]].astype(jnp.float32)
        total = total + thin_c[p][...].astype(jnp.float32) + thin_d[p][...].astype(jnp.float32)
        out_ref[:, pl.ds(OFFSETS[p], WIDTHS[p])] = total.astype(jnp.bfloat16)

    for p in GROUP_A + GROUP_B:
        narrow(p)
    for p in GROUP_A:
        relay_back(p)
    for p in GROUP_A:
        merge(p)
    for p in GROUP_B:
        relay_back(p)
    for p in GROUP_A:
        halfway(p, folds_two, 30, wide_a, wide_b)
    for p in GROUP_B:
        merge(p)
    for p in GROUP_A:
        close_two(p)
    for p in GROUP_B:
        halfway(p, folds_two, 30, wide_a, wide_b)
    for p in GROUP_A:
        halfway(p, folds_one, 34, thin_a, thin_b)
    for p in GROUP_B:
        close_two(p)
    for p in GROUP_A:
        close_one(p)
    for p in GROUP_B:
        halfway(p, folds_one, 34, thin_a, thin_b)
    for p in GROUP_B:
        close_one(p)
    for copy in returned:
        copy.wait_send()


def per_device(
    hidden_in,
    expert_ids,
    gate_coef,
    query_lat,
    kv_cache,
    cache_len,
    gate_weight,
    up_weight,
    down_weight,
):
    bf16, f32 = jnp.bfloat16, jnp.float32
    vmem = lambda *shape, dtype=bf16: pltpu.VMEM(shape, dtype)
    dma = pltpu.SemaphoreType.DMA
    scratch = (
        [vmem(4, 4, 16, w + e) for w, e in zip(WIDTHS, EXTRA)]
        + [vmem(8, 64, w) for w in WIDTHS]
        + [vmem(8, 64, w) for w in WIDTHS]
        + [vmem(8, 64, w) for w in WIDTHS]
        + [vmem(2, 64, w) if o[2] != 1 else vmem(2, 64, 128) for o, w in zip(ORDERS, WIDTHS)]
        + [vmem(2, 64, w) for w in WIDTHS]
        + [vmem(4, 4, 16, w) for w in WIDTHS]
        + [vmem(4, 16, w // 2) for w in WIDTHS] * 2
        + [vmem(4, 16, w) for w in WIDTHS] * 2
        + [vmem(16, w // 2) for w in WIDTHS] * 2
        + [vmem(16, w) for w in WIDTHS] * 2
        + [
            vmem(7168, 512),
            vmem(7168, 512),
            vmem(512, 7168),
            vmem(512, 1024, dtype=f32),
            vmem(512, 512),
            vmem(512, 512),
            vmem(2, 2, 64, 576),
            vmem(2, 2, 576, 128),
            vmem(2, 2, 64, 512),
            dma((PIECES, 38)),
            dma((PIECES, 38)),
            dma((3,)),
            dma((3 * PIECES,)),
            dma((2,)),
            dma((2,)),
            dma((2,)),
        ]
    )
    anywhere = pl.BlockSpec(memory_space=pl.ANY)
    in_vmem = pl.BlockSpec(memory_space=pltpu.VMEM)
    return pl.pallas_call(
        kernel,
        out_shape=(
            jax.ShapeDtypeStruct((16, 64, 512), bf16),
            jax.ShapeDtypeStruct((16, 7168), bf16),
        ),
        in_specs=[pl.BlockSpec(memory_space=pltpu.SMEM), in_vmem, in_vmem] + [anywhere] * 6,
        out_specs=(anywhere, in_vmem),
        scratch_shapes=scratch,
        compiler_params=pltpu.CompilerParams(
            collective_id=0, has_side_effects=True, vmem_limit_bytes=67043328
        ),
        name="moe_step",
    )(
        cache_len,
        expert_ids.T,
        gate_coef.T,
        hidden_in,
        query_lat,
        jnp.swapaxes(kv_cache, 1, 2),
        gate_weight,
        up_weight,
        down_weight,
    )


def solution(mesh):
    in_specs = (
        P(("sec", "dev"), None),
        P(("sec", "dev"), None),
        P(("sec", "dev"), None),
        P(("sec", "dev"), None, None),
        P(("sec", "dev"), None, None),
        P(("sec", "dev")),
        P("dev", None, "sec"),
        P("dev", None, "sec"),
        P("dev", "sec", None),
    )
    out_specs = (P(("sec", "dev"), None, None), P(("sec", "dev"), None))
    return jax.shard_map(
        per_device, mesh=mesh, in_specs=in_specs, out_specs=out_specs, check_vma=False
    )
```

```python
import functools
import math

import jax
import jax.numpy as jnp
from jax import lax
from jax.experimental import pallas as pl
from jax.experimental.pallas import tpu as pltpu
from jax.sharding import PartitionSpec as P

LAT = 512
TOP = 8
MESH = pl.DeviceIdType.MESH
SCALE = 1.0 / math.sqrt(192.0)

WIDTHS = (1280, 1280, 1024, 1024, 1280, 1280)
OFFSETS = (0, 1280, 2560, 3584, 4608, 5888)
EXTRA = (128, 128, 128, 0, 0, 0)
ORDERS = ((0, 1, 2), (2, 0, 1), (1, 2, 0)) * 2
PIECES = 6
GROUP_A, GROUP_B = (0, 1, 2), (3, 4, 5)
TABLE = 128
LANES = 256


def iota(shape, dim):
    return lax.broadcasted_iota(jnp.int32, shape, dim)


def dot(a, b):
    return jnp.dot(a, b, preferred_element_type=jnp.float32)


def dot_nt(a, b):
    return lax.dot_general(a, b, (((1,), (1,)), ((), ())), preferred_element_type=jnp.float32)


def kernel(
    len_ref,
    ids_ref,
    coef_ref,
    hidden_ref,
    query_ref,
    cache_ref,
    gate_ref,
    up_ref,
    down_ref,
    att_ref,
    out_ref,
    *scratch,
):
    len_buf, ids_buf, coef_buf, out_buf, out_sem, small_sem = scratch[106:]
    many = [scratch[i * PIECES : (i + 1) * PIECES] for i in range(15)]
    rows_buf, slot_buf, recv_buf, back_buf, relay_in, relay_out, part_buf = many[:7]
    wide_a, wide_b, wide_c, wide_d, thin_a, thin_b, thin_c, thin_d = many[7:]
    (gate_buf, up_buf, down_buf, acc, hid, hid_p, q_buf, kv_buf, o_buf) = scratch[90:99]
    send_sem, recv_sem, load_sem, own_sem, q_sem, kv_sem, o_sem = scratch[99:106]

    sec = lax.axis_index("sec")
    dev = lax.axis_index("dev")
    core = dev % 2
    pos = (dev // 16, ((dev // 8) % 2) * 2 + sec, (dev // 2) % 4)

    def device(point, which):
        x, y, z = point
        return (y % 2, ((x * 2 + y // 2) * 4 + z) * 2 + which)

    def moved(dim, delta):
        point = list(pos)
        point[dim] = (pos[dim] + delta) % 4
        return tuple(point)

    turn = 1 - 2 * core
    pair = 1 - 2 * (pos[1] % 2)

    barrier = pltpu.get_barrier_semaphore()
    partners = [device(pos, 1 - core)]
    for dim in range(3):
        for delta in (1, -1):
            for which in range(2):
                partners.append(device(moved(dim, delta), which))
    for partner in partners:
        pl.semaphore_signal(barrier, inc=1, device_id=partner, device_id_type=MESH)

    small = [
        pltpu.make_async_copy(ids_ref, ids_buf, small_sem.at[0]),
        pltpu.make_async_copy(coef_ref, coef_buf, small_sem.at[1]),
        pltpu.make_async_copy(len_ref, len_buf, small_sem.at[2]),
    ]
    for copy in small:
        copy.start()
    own = []
    for p in range(PIECES):
        d1, d2, _ = ORDERS[p]
        own.append(
            pltpu.make_async_copy(
                hidden_ref.at[:, pl.ds(OFFSETS[p], WIDTHS[p])],
                rows_buf[p].at[pos[d1], pos[d2], :, pl.ds(0, WIDTHS[p])],
                own_sem.at[p],
            )
        )
        own[p].start()
    loads = [
        pltpu.make_async_copy(gate_ref.at[0], gate_buf, load_sem.at[0]),
        pltpu.make_async_copy(up_ref.at[0], up_buf, load_sem.at[1]),
        pltpu.make_async_copy(down_ref.at[0], down_buf, load_sem.at[2]),
    ]
    for copy in small:
        copy.wait()

    eye = jnp.where(iota((16, 16), 0) == iota((16, 16), 1), 1.0, 0.0).astype(jnp.bfloat16)
    names = dot_nt(eye, ids_buf[...].astype(jnp.float32).astype(jnp.bfloat16))
    coefs = dot_nt(eye, coef_buf[...].astype(jnp.bfloat16))
    lane = iota((16, TABLE), 1)
    expert_of = (lane >> 1).astype(jnp.float32)
    hit = jnp.zeros((16, TABLE), jnp.float32)
    weight = jnp.zeros((16, TABLE), jnp.float32)
    for k in range(TOP):
        match = names[:, k : k + 1] == expert_of
        hit = hit + jnp.where(match, 1.0, 0.0)
        weight = weight + jnp.where(match, coefs[:, k : k + 1], 0.0)
    low = (iota((16, 16), 1) < iota((16, 16), 0)) & ((iota((16, 16), 1) >> 3) == (iota((16, 16), 0) >> 3))
    rank = dot(jnp.where(low, 1.0, 0.0).astype(jnp.bfloat16), hit.astype(jnp.bfloat16))
    table = jnp.where(rank == (lane & 1).astype(jnp.float32), weight, 0.0).astype(jnp.bfloat16)
    for p in GROUP_A:
        d1, d2, _ = ORDERS[p]
        rows_buf[p][pos[d1], pos[d2], :, pl.ds(WIDTHS[p], TABLE)] = table

    for p in range(PIECES):
        own[p].wait()
    pl.semaphore_wait(barrier, len(partners))

    def remote(src, dst, p, send, recv, target):
        return pltpu.make_async_remote_copy(
            src_ref=src,
            dst_ref=dst,
            send_sem=send_sem.at[p, send],
            recv_sem=recv_sem.at[p, recv],
            device_id=target,
            device_id_type=MESH,
        )

    def arrived(dst, p, recv):
        remote(dst, dst, p, 0, recv, device(pos, 1 - core)).wait_recv()

    def q_copy(step, slot):
        return pltpu.make_async_copy(query_ref.at[pl.ds(step * 2, 2)], q_buf.at[slot], q_sem.at[slot])

    def kv_copy(step, slot):
        return pltpu.make_async_copy(cache_ref.at[pl.ds(step * 2, 2)], kv_buf.at[slot], kv_sem.at[slot])

    def o_copy(step, slot):
        return pltpu.make_async_copy(o_buf.at[slot], att_ref.at[pl.ds(step * 2, 2)], o_sem.at[slot])

    def attend(step, carry):
        slot = step % 2
        q_copy(step, slot).wait()
        kv_copy(step, slot).wait()

        @pl.when(step >= 2)
        def _():
            o_copy(step, slot).wait()

        for i in range(2):
            keys = kv_buf[slot, i]
            scores = dot(q_buf[slot, i], keys) * SCALE
            visible = iota((64, 128), 1) < len_buf[step * 2 + i]
            scores = jnp.where(visible, scores, -1e30)
            exponent = jnp.exp(scores - jnp.max(scores, axis=1, keepdims=True))
            weights = (exponent / jnp.sum(exponent, axis=1, keepdims=True)).astype(jnp.bfloat16)
            o_buf[slot, i] = dot_nt(weights, keys[:LAT, :]).astype(jnp.bfloat16)
        o_copy(step, slot).start()

        @pl.when(step + 2 < 8)
        def _():
            q_copy(step + 2, slot).start()
            kv_copy(step + 2, slot).start()

        return carry

    for step in range(2):
        q_copy(step, step).start()
        kv_copy(step, step).start()

    def ring(p, dim, base, block):
        half = WIDTHS[p] // 2
        rest = half + EXTRA[p]
        here, up, down = pos[dim], (pos[dim] + 1) % 4, (pos[dim] + 3) % 4
        above, below = device(moved(dim, 1), core), device(moved(dim, -1), core)
        first = [
            remote(block(here), block(here), p, base, base, above),
            remote(block(here), block(here), p, base + 1, base + 1, below),
        ]
        low_part = lambda i: block(i, pl.ds(0, half))
        high_part = lambda i: block(i, pl.ds(half, rest))
        second = [
            remote(low_part(down), low_part(down), p, base + 2, base + 2, above),
            remote(high_part(up), high_part(up), p, base + 3, base + 3, below),
        ]
        far = (pos[dim] + 2) % 4
        waits = [
            lambda: arrived(block(down), p, base),
            lambda: arrived(block(up), p, base + 1),
            lambda: arrived(low_part(far), p, base + 2),
            lambda: arrived(high_part(far), p, base + 3),
        ]
        return first, second, waits

    rings_one, rings_two = [], []
    for p in range(PIECES):
        d1, d2, _ = ORDERS[p]

        def block_one(i, columns=slice(None), p=p, d2=d2):
            return rows_buf[p].at[i, pos[d2], :, columns]

        def block_two(i, columns=slice(None), p=p):
            return rows_buf[p].at[:, i, :, columns]

        rings_one.append(ring(p, d1, 0, block_one))
        rings_two.append(ring(p, d2, 4, block_two))

    def begin(rings, group):
        for p in group:
            for copy in rings[p][0]:
                copy.start()

    def turn_round(rings, group):
        for p in group:
            _, second, waits = rings[p]
            for i in range(2):
                waits[i]()
                second[i].start()

    def finish(rings, p):
        waits = rings[p][2]
        waits[2]()
        waits[3]()

    def drain(rings):
        for first, second, _ in rings:
            for copy in first + second:
                copy.wait_send()

    def chooser(p):
        n = iota((512, TABLE), 0)
        other, which, slot = n >> 7, (n >> 6) & 1, n & 1
        if ORDERS[p][2] == 2:
            expert = ((pos[0] * 2 + pos[1] // 2) * 4 + other) * 2 + which
        elif ORDERS[p][2] == 1:
            expert = ((pos[0] * 2 + (other >> 1)) * 4 + pos[2]) * 2 + which
        else:
            expert = ((other * 2 + pos[1] // 2) * 4 + pos[2]) * 2 + which
        return jnp.where(iota((512, TABLE), 1) == expert * 2 + slot, 1.0, 0.0).astype(jnp.bfloat16)

    def table_of(p):
        first = p % 3
        return rows_buf[first][:, :, :, pl.ds(WIDTHS[first], TABLE)].reshape(256, TABLE)

    def columns_of(i):
        return pl.ds(pl.multiple_of(i * LANES, LANES), LANES)

    sent = [[] for _ in range(PIECES)]
    local = [None] * PIECES

    def spread(p):
        _, _, d3 = ORDERS[p]
        finish(rings_two, p)
        hot = dot_nt(chooser(p), table_of(p))
        near = ((iota((512, 256), 0) & 63) >> 1) == (iota((512, 256), 1) >> 3)
        picker = jnp.where(near & (hot != 0.0), 1.0, 0.0).astype(jnp.bfloat16)

        def pick(i, carry):
            block = rows_buf[p][:, :, :, columns_of(i)].reshape(256, LANES)
            slot_buf[p][:, :, columns_of(i)] = dot(picker, block).astype(jnp.bfloat16).reshape(8, 64, LANES)
            return carry

        lax.fori_loop(0, WIDTHS[p] // LANES, pick, 0)

        def send(copy):
            copy.start()
            sent[p].append(copy)

        here = pos[d3]
        far = (here + 2) % 4
        mine = core * 4 + here
        if d3 != 1:
            for which, delta in ((0, 1), (1, -1)):
                target = device(moved(d3, delta), which)
                send(remote(slot_buf[p].at[far * 2 + which], relay_in[p].at[core], p, 12 + which, 16 + core, target))
            deltas = ((1, 10), (-1, 8))
        else:
            deltas = ((-pair, 8), (pair, 10))
        for delta, base in deltas:
            there = (here + delta) % 4
            for which in range(2):
                target = device(moved(d3, delta), which)
                send(remote(slot_buf[p].at[there * 2 + which], recv_buf[p].at[mine], p, base + which, 8 + mine, target))
        send(remote(slot_buf[p].at[here * 2 + 1 - core], recv_buf[p].at[mine], p, 14, 8 + mine, device(pos, 1 - core)))
        local[p] = pltpu.make_async_copy(slot_buf[p].at[here * 2 + core], recv_buf[p].at[mine], own_sem.at[PIECES + p])
        local[p].start()

    def relay(p):
        _, _, d3 = ORDERS[p]
        here = pos[d3]
        for c in range(2):
            if d3 != 1:
                arrived(relay_in[p].at[c], p, 16 + c)
                entry = c * 4 + (here - turn) % 4
                copy = remote(relay_in[p].at[c], recv_buf[p].at[entry], p, 18 + c, 8 + entry, device(moved(d3, turn), core))
            else:
                entry = c * 4 + (here - pair) % 4
                arrived(recv_buf[p].at[entry], p, 8 + entry)
                copy = remote(recv_buf[p].at[entry], recv_buf[p].at[entry], p, 18 + c, 8 + entry, device(moved(d3, pair), core))
            copy.start()
            sent[p].append(copy)

    def collect(p):
        _, _, d3 = ORDERS[p]
        here = pos[d3]
        for c in range(2):
            for delta in (1, 3, 2) if d3 != 1 else (pair, 2):
                entry = c * 4 + (here + delta) % 4
                arrived(recv_buf[p].at[entry], p, 8 + entry)
        entry = (1 - core) * 4 + here
        arrived(recv_buf[p].at[entry], p, 8 + entry)
        local[p].wait()
        for copy in sent[p]:
            copy.wait_send()

    def source_row(p, i):
        z, x, y, q = i >> 6, (i >> 4) & 3, (i >> 2) & 3, i & 3
        if ORDERS[p][2] == 1:
            return y * 64 + z * 16 + x * 4 + q
        return x * 64 + y * 16 + z * 4 + q

    def widen(p):
        held = recv_buf[p]
        if ORDERS[p][2] != 2:
            held = slot_buf[p]
            order = jnp.where(source_row(p, iota((256, 256), 0)) == iota((256, 256), 1), 1.0, 0.0).astype(jnp.bfloat16)

            def straighten(i, carry):
                for c in range(2):
                    block = recv_buf[p][pl.ds(c * 4, 4), :, columns_of(i)].reshape(256, LANES)
                    slot_buf[p][pl.ds(c * 4, 4), :, columns_of(i)] = dot(order, block).astype(jnp.bfloat16).reshape(4, 64, LANES)
                return carry

            lax.fori_loop(0, WIDTHS[p] // LANES, straighten, 0)
        block = held[...].reshape(512, WIDTHS[p])
        deep = slice(OFFSETS[p], OFFSETS[p] + WIDTHS[p])
        for n in range(2):
            for base, buf in ((0, gate_buf), (512, up_buf)):
                product = dot(block, buf[deep, n * 256 : n * 256 + 256])
                columns = slice(base + n * 256, base + n * 256 + 256)
                if p == 0:
                    acc[:, columns] = product
                else:
                    acc[:, columns] += product

    def activate(i, carry):
        rows = pl.ds(pl.multiple_of(i * 64, 64), 64)
        gate_val = acc[rows, 0:512]
        hid[rows, :] = ((gate_val / (1.0 + jnp.exp(-gate_val))) * acc[rows, 512:1024]).astype(jnp.bfloat16)
        return carry

    begin(rings_one, GROUP_A)
    begin(rings_one, GROUP_B)
    for load in loads:
        load.start()
    lax.fori_loop(0, 1, attend, 0)
    turn_round(rings_one, GROUP_A)
    turn_round(rings_one, GROUP_B)
    lax.fori_loop(1, 2, attend, 0)
    for p in GROUP_A + GROUP_B:
        finish(rings_one, p)
        begin(rings_two, (p,))
    lax.fori_loop(2, 5, attend, 0)
    turn_round(rings_two, GROUP_A)
    lax.fori_loop(5, 6, attend, 0)
    turn_round(rings_two, GROUP_B)
    for p in GROUP_A:
        spread(p)
    lax.fori_loop(6, 8, attend, 0)
    for p in GROUP_A:
        relay(p)
    for p in GROUP_B:
        spread(p)
    loads[0].wait()
    loads[1].wait()
    for p in GROUP_A:
        collect(p)
        widen(p)
        relay(p + 3)
    for p in GROUP_B:
        collect(p)
        widen(p)
    drain(rings_one)
    drain(rings_two)
    for step in (6, 7):
        o_copy(step, step % 2).wait()
    loads[2].wait()
    lax.fori_loop(0, 8, activate, 0)

    returned = []

    def give(copy):
        copy.start()
        returned.append(copy)

    def narrow(p):
        _, _, d3 = ORDERS[p]
        if d3 == 2:
            hid_p[...] = hid[...]
        else:
            order = jnp.where(source_row(p, iota((256, 256), 1)) == iota((256, 256), 0), 1.0, 0.0).astype(jnp.bfloat16)
            for c in range(2):
                hid_p[c * 256 : c * 256 + 256, :] = dot(order, hid[c * 256 : c * 256 + 256, :]).astype(jnp.bfloat16)

        def shrink(i, carry):
            deep = pl.ds(pl.multiple_of(OFFSETS[p] + i * LANES, LANES), LANES)
            recv_buf[p][:, :, columns_of(i)] = dot(hid_p[...], down_buf[:, deep]).astype(jnp.bfloat16).reshape(8, 64, LANES)
            return carry

        lax.fori_loop(0, WIDTHS[p] // LANES, shrink, 0)

    def send_back(p):
        _, _, d3 = ORDERS[p]
        here = pos[d3]
        far = (here + 2) % 4
        entry = here * 2 + core
        step = turn if d3 != 1 else pair
        for c in range(2):
            give(remote(recv_buf[p].at[c * 4 + far], relay_out[p].at[c], p, 24 + c, 28 + c, device(moved(d3, step), core)))
        for delta, base in ((1, 20), (-1, 22)):
            there = (here + delta) % 4
            for c in range(2):
                give(remote(recv_buf[p].at[c * 4 + there], back_buf[p].at[entry], p, base + c, 20 + entry, device(moved(d3, delta), c)))
        give(remote(recv_buf[p].at[(1 - core) * 4 + here], back_buf[p].at[entry], p, 26, 20 + entry, device(pos, 1 - core)))
        local[p] = pltpu.make_async_copy(recv_buf[p].at[core * 4 + here], back_buf[p].at[entry], own_sem.at[2 * PIECES + p])
        local[p].start()

    def relay_back(p):
        _, _, d3 = ORDERS[p]
        here = pos[d3]
        step = turn if d3 != 1 else -pair
        origin = -turn if d3 != 1 else pair
        entry = ((here + origin) % 4) * 2 + core
        for c in range(2):
            arrived(relay_out[p].at[c], p, 28 + c)
            give(remote(relay_out[p].at[c], back_buf[p].at[entry], p, 28 + c, 20 + entry, device(moved(d3, step), c)))

    def fold(p, dim, base, block, bufs):
        half = WIDTHS[p] // 2
        rest = half
        here, up, down, far = pos[dim], (pos[dim] + 1) % 4, (pos[dim] + 3) % 4, (pos[dim] + 2) % 4
        above, below = device(moved(dim, 1), core), device(moved(dim, -1), core)
        low_part = lambda i: block(i, pl.ds(0, half))
        high_part = lambda i: block(i, pl.ds(half, rest))
        first = [
            remote(low_part(far), bufs[0], p, base, base, above),
            remote(high_part(far), bufs[1], p, base + 1, base + 1, below),
        ]
        second = [
            remote(block(up), bufs[2], p, base + 2, base + 2, above),
            remote(block(down), bufs[3], p, base + 3, base + 3, below),
        ]
        return first, second, low_part(up), high_part(down)

    folds_two, folds_one = [None] * PIECES, [None] * PIECES

    def merge(p):
        d1, d2, d3 = ORDERS[p]
        here = pos[d3]
        arrivals = [(here * 2 + 1 - core)]
        for delta in (1, 2, 3):
            for which in range(2):
                arrivals.append(((here + delta) % 4) * 2 + which)
        for entry in arrivals:
            arrived(back_buf[p].at[entry], p, 20 + entry)
        local[p].wait()
        near = ((iota((256, 512), 1) & 63) >> 1) == (iota((256, 512), 0) >> 3)
        mixer = jnp.where(near, dot_nt(table_of(p), chooser(p)), 0.0).astype(jnp.bfloat16)

        def mix(i, carry):
            block = back_buf[p][:, :, columns_of(i)].reshape(512, LANES)
            part_buf[p][:, :, :, columns_of(i)] = dot(mixer, block).astype(jnp.bfloat16).reshape(4, 4, 16, LANES)
            return carry

        lax.fori_loop(0, WIDTHS[p] // LANES, mix, 0)
        block_two = lambda i, columns=slice(None): part_buf[p].at[:, i, :, columns]
        block_one = lambda i, columns=slice(None): part_buf[p].at[i, pos[d2], :, columns]
        folds_two[p] = fold(p, d2, 30, block_two, (wide_a[p], wide_b[p], wide_c[p], wide_d[p]))
        folds_one[p] = fold(p, d1, 34, block_one, (thin_a[p], thin_b[p], thin_c[p], thin_d[p]))
        for copy in folds_two[p][0]:
            give(copy)

    def add_into(ref, *others):
        total = ref[...].astype(jnp.float32)
        for other in others:
            total = total + other[...].astype(jnp.float32)
        ref[...] = total.astype(jnp.bfloat16)

    def halfway(p, folds, base, low_buf, high_buf):
        _, second, low_up, high_down = folds[p]
        arrived(low_buf[p], p, base)
        add_into(low_up, low_buf[p])
        give(second[0])
        arrived(high_buf[p], p, base + 1)
        add_into(high_down, high_buf[p])
        give(second[1])

    def close_two(p):
        arrived(wide_c[p], p, 32)
        arrived(wide_d[p], p, 33)
        add_into(part_buf[p].at[:, pos[ORDERS[p][1]]], wide_c[p], wide_d[p])
        for copy in folds_one[p][0]:
            give(copy)

    outs = []

    def close_one(p):
        d1, d2, _ = ORDERS[p]
        arrived(thin_c[p], p, 36)
        arrived(thin_d[p], p, 37)
        total = part_buf[p][pos[d1], pos[d2]].astype(jnp.float32)
        total = total + thin_c[p][...].astype(jnp.float32) + thin_d[p][...].astype(jnp.float32)
        columns = pl.ds(OFFSETS[p], WIDTHS[p])
        out_buf[:, columns] = total.astype(jnp.bfloat16)
        outs.append(pltpu.make_async_copy(out_buf.at[:, columns], out_ref.at[:, columns], out_sem.at[p]))
        outs[-1].start()

    for p in GROUP_A:
        narrow(p)
        send_back(p)
    for p in GROUP_B:
        narrow(p)
    for p in GROUP_A:
        relay_back(p)
    for p in GROUP_B:
        send_back(p)
    for p in GROUP_A:
        merge(p)
    for p in GROUP_B:
        relay_back(p)
    for p in GROUP_A:
        halfway(p, folds_two, 30, wide_a, wide_b)
    for p in GROUP_B:
        merge(p)
    for p in GROUP_A:
        close_two(p)
    for p in GROUP_B:
        halfway(p, folds_two, 30, wide_a, wide_b)
    for p in GROUP_A:
        halfway(p, folds_one, 34, thin_a, thin_b)
    for p in GROUP_B:
        close_two(p)
    for p in GROUP_A:
        close_one(p)
    for p in GROUP_B:
        halfway(p, folds_one, 34, thin_a, thin_b)
    for p in GROUP_B:
        close_one(p)
    for copy in outs:
        copy.wait()
    for copy in returned:
        copy.wait_send()


def hand_over(att_in, out_in, att_out, out_out, att_buf, out_buf, in_sem, out_sem):
    parts = [(out_in, out_buf, out_out)]
    for i in range(4):
        rows = pl.ds(i * 4, 4)
        parts.append((att_in.at[rows], att_buf.at[rows], att_out.at[rows]))
    takes = [pltpu.make_async_copy(a, b, in_sem.at[i]) for i, (a, b, _) in enumerate(parts)]
    gives = [pltpu.make_async_copy(b, c, out_sem.at[i]) for i, (_, b, c) in enumerate(parts)]
    for take in takes:
        take.start()
    for take, give in zip(takes, gives):
        take.wait()
        give.start()
    for give in gives:
        give.wait()


def per_device(
    hidden_in,
    expert_ids,
    gate_coef,
    query_lat,
    kv_cache,
    cache_len,
    gate_weight,
    up_weight,
    down_weight,
):
    bf16, f32 = jnp.bfloat16, jnp.float32
    vmem = lambda *shape, dtype=bf16: pltpu.VMEM(shape, dtype)
    dma = pltpu.SemaphoreType.DMA
    scratch = (
        [vmem(4, 4, 16, w + e) for w, e in zip(WIDTHS, EXTRA)]
        + [vmem(8, 64, w) for w in WIDTHS]
        + [vmem(8, 64, w) for w in WIDTHS]
        + [vmem(8, 64, w) for w in WIDTHS]
        + [vmem(2, 64, w) if o[2] != 1 else vmem(2, 64, 128) for o, w in zip(ORDERS, WIDTHS)]
        + [vmem(2, 64, w) for w in WIDTHS]
        + [vmem(4, 4, 16, w) for w in WIDTHS]
        + [vmem(4, 16, w // 2) for w in WIDTHS] * 2
        + [vmem(4, 16, w) for w in WIDTHS] * 2
        + [vmem(16, w // 2) for w in WIDTHS] * 2
        + [vmem(16, w) for w in WIDTHS] * 2
        + [
            vmem(7168, 512),
            vmem(7168, 512),
            vmem(512, 7168),
            vmem(512, 1024, dtype=f32),
            vmem(512, 512),
            vmem(512, 512),
            vmem(2, 2, 64, 576),
            vmem(2, 2, 576, 128),
            vmem(2, 2, 64, 512),
            dma((PIECES, 38)),
            dma((PIECES, 38)),
            dma((3,)),
            dma((3 * PIECES,)),
            dma((2,)),
            dma((2,)),
            dma((2,)),
            pltpu.SMEM((16,), jnp.int32),
            vmem(8, 16, dtype=jnp.int32),
            vmem(8, 16, dtype=f32),
            vmem(16, 7168),
            dma((PIECES,)),
            dma((3,)),
        ]
    )
    anywhere = pl.BlockSpec(memory_space=pl.ANY)
    attention, routed = pl.pallas_call(
        kernel,
        out_shape=(
            jax.ShapeDtypeStruct((16, 64, 512), bf16),
            jax.ShapeDtypeStruct((16, 7168), bf16),
        ),
        in_specs=[anywhere] * 9,
        out_specs=(anywhere, anywhere),
        scratch_shapes=scratch,
        compiler_params=pltpu.CompilerParams(
            collective_id=0, has_side_effects=True, vmem_limit_bytes=67043328
        ),
        name="moe_step",
    )(
        cache_len,
        expert_ids.T,
        gate_coef.T,
        hidden_in,
        query_lat,
        jnp.swapaxes(kv_cache, 1, 2),
        gate_weight,
        up_weight,
        down_weight,
    )
    return pl.pallas_call(
        hand_over,
        out_shape=(
            jax.ShapeDtypeStruct((16, 64, 512), bf16),
            jax.ShapeDtypeStruct((16, 7168), bf16),
        ),
        in_specs=[anywhere] * 2,
        out_specs=(anywhere, anywhere),
        scratch_shapes=[vmem(16, 64, 512), vmem(16, 7168), dma((5,)), dma((5,))],
        name="hand_over",
    )(attention, routed)


def solution(mesh):
    in_specs = (
        P(("sec", "dev"), None),
        P(("sec", "dev"), None),
        P(("sec", "dev"), None),
        P(("sec", "dev"), None, None),
        P(("sec", "dev"), None, None),
        P(("sec", "dev")),
        P("dev", None, "sec"),
        P("dev", None, "sec"),
        P("dev", "sec", None),
    )
    out_specs = (P(("sec", "dev"), None, None), P(("sec", "dev"), None))
    return jax.shard_map(
        per_device, mesh=mesh, in_specs=in_specs, out_specs=out_specs, check_vma=False
    )
```

```python
import functools
import math

import jax
import jax.numpy as jnp
from jax import lax
from jax.experimental import pallas as pl
from jax.experimental.pallas import tpu as pltpu
from jax.sharding import PartitionSpec as P

LAT = 512
TOP = 8
MESH = pl.DeviceIdType.MESH
SCALE = 1.0 / math.sqrt(192.0)

WIDTHS = (1280, 1280, 1024, 1024, 1280, 1280)
OFFSETS = (0, 1280, 2560, 3584, 4608, 5888)
EXTRA = (128, 128, 128, 0, 0, 0)
ORDERS = ((0, 1, 2), (2, 0, 1), (1, 2, 0)) * 2
PIECES = 6
GROUP_A, GROUP_B = (0, 1, 2), (3, 4, 5)
TABLE = 128
LANES = 256


def iota(shape, dim):
    return lax.broadcasted_iota(jnp.int32, shape, dim)


def dot(a, b):
    return jnp.dot(a, b, preferred_element_type=jnp.float32)


def dot_nt(a, b):
    return lax.dot_general(a, b, (((1,), (1,)), ((), ())), preferred_element_type=jnp.float32)


def kernel(
    len_ref,
    ids_ref,
    coef_ref,
    hidden_ref,
    query_ref,
    cache_ref,
    gate_ref,
    up_ref,
    down_ref,
    att_ref,
    out_ref,
    *scratch,
):
    len_buf, ids_buf, coef_buf, out_buf, out_sem, small_sem = scratch[106:]
    many = [scratch[i * PIECES : (i + 1) * PIECES] for i in range(15)]
    rows_buf, slot_buf, recv_buf, back_buf, relay_in, relay_out, part_buf = many[:7]
    wide_a, wide_b, wide_c, wide_d, thin_a, thin_b, thin_c, thin_d = many[7:]
    (gate_buf, up_buf, down_buf, acc, hid, hid_p, q_buf, kv_buf, o_buf) = scratch[90:99]
    send_sem, recv_sem, load_sem, own_sem, q_sem, kv_sem, o_sem = scratch[99:106]

    sec = lax.axis_index("sec")
    dev = lax.axis_index("dev")
    core = dev % 2
    pos = (dev // 16, ((dev // 8) % 2) * 2 + sec, (dev // 2) % 4)

    def device(point, which):
        x, y, z = point
        return (y % 2, ((x * 2 + y // 2) * 4 + z) * 2 + which)

    def moved(dim, delta):
        point = list(pos)
        point[dim] = (pos[dim] + delta) % 4
        return tuple(point)

    turn = 1 - 2 * core
    pair = 1 - 2 * (pos[1] % 2)

    barrier = pltpu.get_barrier_semaphore()
    partners = [device(pos, 1 - core)]
    for dim in range(3):
        for delta in (1, -1):
            for which in range(2):
                partners.append(device(moved(dim, delta), which))
    for partner in partners:
        pl.semaphore_signal(barrier, inc=1, device_id=partner, device_id_type=MESH)

    small = [
        pltpu.make_async_copy(ids_ref, ids_buf, small_sem.at[0]),
        pltpu.make_async_copy(coef_ref, coef_buf, small_sem.at[1]),
        pltpu.make_async_copy(len_ref, len_buf, small_sem.at[2]),
    ]
    for copy in small:
        copy.start()
    own = []
    for p in range(PIECES):
        d1, d2, _ = ORDERS[p]
        own.append(
            pltpu.make_async_copy(
                hidden_ref.at[:, pl.ds(OFFSETS[p], WIDTHS[p])],
                rows_buf[p].at[pos[d1], pos[d2], :, pl.ds(0, WIDTHS[p])],
                own_sem.at[p],
            )
        )
        own[p].start()
    loads = [
        pltpu.make_async_copy(gate_ref.at[0], gate_buf, load_sem.at[0]),
        pltpu.make_async_copy(up_ref.at[0], up_buf, load_sem.at[1]),
        pltpu.make_async_copy(down_ref.at[0], down_buf, load_sem.at[2]),
    ]
    for copy in small:
        copy.wait()

    eye = jnp.where(iota((16, 16), 0) == iota((16, 16), 1), 1.0, 0.0).astype(jnp.bfloat16)
    names = dot_nt(eye, ids_buf[...].astype(jnp.float32).astype(jnp.bfloat16))
    coefs = dot_nt(eye, coef_buf[...].astype(jnp.bfloat16))
    lane = iota((16, TABLE), 1)
    expert_of = (lane >> 1).astype(jnp.float32)
    hit = jnp.zeros((16, TABLE), jnp.float32)
    weight = jnp.zeros((16, TABLE), jnp.float32)
    for k in range(TOP):
        match = names[:, k : k + 1] == expert_of
        hit = hit + jnp.where(match, 1.0, 0.0)
        weight = weight + jnp.where(match, coefs[:, k : k + 1], 0.0)
    low = (iota((16, 16), 1) < iota((16, 16), 0)) & ((iota((16, 16), 1) >> 3) == (iota((16, 16), 0) >> 3))
    rank = dot(jnp.where(low, 1.0, 0.0).astype(jnp.bfloat16), hit.astype(jnp.bfloat16))
    table = jnp.where(rank == (lane & 1).astype(jnp.float32), weight, 0.0).astype(jnp.bfloat16)
    for p in GROUP_A:
        d1, d2, _ = ORDERS[p]
        rows_buf[p][pos[d1], pos[d2], :, pl.ds(WIDTHS[p], TABLE)] = table

    for p in range(PIECES):
        own[p].wait()
    pl.semaphore_wait(barrier, len(partners))

    def remote(src, dst, p, send, recv, target):
        return pltpu.make_async_remote_copy(
            src_ref=src,
            dst_ref=dst,
            send_sem=send_sem.at[p, send],
            recv_sem=recv_sem.at[p, recv],
            device_id=target,
            device_id_type=MESH,
        )

    def arrived(dst, p, recv):
        remote(dst, dst, p, 0, recv, device(pos, 1 - core)).wait_recv()

    def q_copy(step, slot):
        return pltpu.make_async_copy(query_ref.at[pl.ds(step * 2, 2)], q_buf.at[slot], q_sem.at[slot])

    def kv_copy(step, slot):
        return pltpu.make_async_copy(cache_ref.at[pl.ds(step * 2, 2)], kv_buf.at[slot], kv_sem.at[slot])

    def o_copy(step, slot):
        return pltpu.make_async_copy(o_buf.at[slot], att_ref.at[pl.ds(step * 2, 2)], o_sem.at[slot])

    def attend(step, carry):
        slot = step % 2
        q_copy(step, slot).wait()
        kv_copy(step, slot).wait()

        @pl.when(step >= 2)
        def _():
            o_copy(step, slot).wait()

        for i in range(2):
            keys = kv_buf[slot, i]
            scores = dot(q_buf[slot, i], keys) * SCALE
            visible = iota((64, 128), 1) < len_buf[step * 2 + i]
            scores = jnp.where(visible, scores, -1e30)
            exponent = jnp.exp(scores - jnp.max(scores, axis=1, keepdims=True))
            weights = (exponent / jnp.sum(exponent, axis=1, keepdims=True)).astype(jnp.bfloat16)
            o_buf[slot, i] = dot_nt(weights, keys[:LAT, :]).astype(jnp.bfloat16)
        o_copy(step, slot).start()

        @pl.when(step + 2 < 8)
        def _():
            q_copy(step + 2, slot).start()
            kv_copy(step + 2, slot).start()

        return carry

    for step in range(2):
        q_copy(step, step).start()
        kv_copy(step, step).start()

    def ring(p, dim, base, late, block):
        half = WIDTHS[p] // 2
        rest = half + EXTRA[p]
        here, up, down = pos[dim], (pos[dim] + 1) % 4, (pos[dim] + 3) % 4
        above, below = device(moved(dim, 1), core), device(moved(dim, -1), core)
        low_part = lambda i: block(i, pl.ds(0, half))
        high_part = lambda i: block(i, pl.ds(half, rest))
        first = [
            remote(low_part(here), low_part(here), p, base, base, above),
            remote(high_part(here), high_part(here), p, base + 1, base + 1, below),
            remote(high_part(here), high_part(here), p, late, late, above),
            remote(low_part(here), low_part(here), p, late + 1, late + 1, below),
        ]
        second = [
            remote(low_part(down), low_part(down), p, base + 2, base + 2, above),
            remote(high_part(up), high_part(up), p, base + 3, base + 3, below),
        ]
        far = (pos[dim] + 2) % 4
        waits = [
            lambda: arrived(low_part(down), p, base),
            lambda: arrived(high_part(up), p, base + 1),
            lambda: arrived(high_part(down), p, late),
            lambda: arrived(low_part(up), p, late + 1),
            lambda: arrived(low_part(far), p, base + 2),
            lambda: arrived(high_part(far), p, base + 3),
        ]
        return first, second, waits

    rings_one, rings_two = [], []
    for p in range(PIECES):
        d1, d2, _ = ORDERS[p]

        def block_one(i, columns=slice(None), p=p, d2=d2):
            return rows_buf[p].at[i, pos[d2], :, columns]

        def block_two(i, columns=slice(None), p=p):
            return rows_buf[p].at[:, i, :, columns]

        rings_one.append(ring(p, d1, 0, 38, block_one))
        rings_two.append(ring(p, d2, 4, 40, block_two))

    def begin(rings, group):
        for p in group:
            for copy in rings[p][0]:
                copy.start()

    def turn_round(rings, group):
        for p in group:
            _, second, waits = rings[p]
            for i in range(2):
                waits[i]()
                second[i].start()

    def finish(rings, p):
        waits = rings[p][2]
        for wait in waits[2:]:
            wait()

    def drain(rings):
        for first, second, _ in rings:
            for copy in first + second:
                copy.wait_send()

    def chooser(p):
        n = iota((512, TABLE), 0)
        other, which, slot = n >> 7, (n >> 6) & 1, n & 1
        if ORDERS[p][2] == 2:
            expert = ((pos[0] * 2 + pos[1] // 2) * 4 + other) * 2 + which
        elif ORDERS[p][2] == 1:
            expert = ((pos[0] * 2 + (other >> 1)) * 4 + pos[2]) * 2 + which
        else:
            expert = ((other * 2 + pos[1] // 2) * 4 + pos[2]) * 2 + which
        return jnp.where(iota((512, TABLE), 1) == expert * 2 + slot, 1.0, 0.0).astype(jnp.bfloat16)

    def table_of(p):
        first = p % 3
        return rows_buf[first][:, :, :, pl.ds(WIDTHS[first], TABLE)].reshape(256, TABLE)

    def columns_of(i):
        return pl.ds(pl.multiple_of(i * LANES, LANES), LANES)

    sent = [[] for _ in range(PIECES)]
    local = [None] * PIECES

    def spread(p):
        _, _, d3 = ORDERS[p]
        finish(rings_two, p)
        hot = dot_nt(chooser(p), table_of(p))
        near = ((iota((512, 256), 0) & 63) >> 1) == (iota((512, 256), 1) >> 3)
        picker = jnp.where(near & (hot != 0.0), 1.0, 0.0).astype(jnp.bfloat16)

        def pick(i, carry):
            block = rows_buf[p][:, :, :, columns_of(i)].reshape(256, LANES)
            slot_buf[p][:, :, columns_of(i)] = dot(picker, block).astype(jnp.bfloat16).reshape(8, 64, LANES)
            return carry

        lax.fori_loop(0, WIDTHS[p] // LANES, pick, 0)

        def send(copy):
            copy.start()
            sent[p].append(copy)

        here = pos[d3]
        far = (here + 2) % 4
        mine = core * 4 + here
        if d3 != 1:
            for which, delta in ((0, 1), (1, -1)):
                target = device(moved(d3, delta), which)
                send(remote(slot_buf[p].at[far * 2 + which], relay_in[p].at[core], p, 12 + which, 16 + core, target))
            deltas = ((1, 10), (-1, 8))
        else:
            deltas = ((-pair, 8), (pair, 10))
        for delta, base in deltas:
            there = (here + delta) % 4
            for which in range(2):
                target = device(moved(d3, delta), which)
                send(remote(slot_buf[p].at[there * 2 + which], recv_buf[p].at[mine], p, base + which, 8 + mine, target))
        send(remote(slot_buf[p].at[here * 2 + 1 - core], recv_buf[p].at[mine], p, 14, 8 + mine, device(pos, 1 - core)))
        local[p] = pltpu.make_async_copy(slot_buf[p].at[here * 2 + core], recv_buf[p].at[mine], own_sem.at[PIECES + p])
        local[p].start()

    def relay(p):
        _, _, d3 = ORDERS[p]
        here = pos[d3]
        for c in range(2):
            if d3 != 1:
                arrived(relay_in[p].at[c], p, 16 + c)
                entry = c * 4 + (here - turn) % 4
                copy = remote(relay_in[p].at[c], recv_buf[p].at[entry], p, 18 + c, 8 + entry, device(moved(d3, turn), core))
            else:
                entry = c * 4 + (here - pair) % 4
                arrived(recv_buf[p].at[entry], p, 8 + entry)
                copy = remote(recv_buf[p].at[entry], recv_buf[p].at[entry], p, 18 + c, 8 + entry, device(moved(d3, pair), core))
            copy.start()
            sent[p].append(copy)

    def collect(p):
        _, _, d3 = ORDERS[p]
        here = pos[d3]
        for c in range(2):
            for delta in (1, 3, 2) if d3 != 1 else (pair, 2):
                entry = c * 4 + (here + delta) % 4
                arrived(recv_buf[p].at[entry], p, 8 + entry)
        entry = (1 - core) * 4 + here
        arrived(recv_buf[p].at[entry], p, 8 + entry)
        local[p].wait()
        for copy in sent[p]:
            copy.wait_send()

    def source_row(p, i):
        z, x, y, q = i >> 6, (i >> 4) & 3, (i >> 2) & 3, i & 3
        if ORDERS[p][2] == 1:
            return y * 64 + z * 16 + x * 4 + q
        return x * 64 + y * 16 + z * 4 + q

    def widen(p):
        held = recv_buf[p]
        if ORDERS[p][2] != 2:
            held = slot_buf[p]
            order = jnp.where(source_row(p, iota((256, 256), 0)) == iota((256, 256), 1), 1.0, 0.0).astype(jnp.bfloat16)

            def straighten(i, carry):
                for c in range(2):
                    block = recv_buf[p][pl.ds(c * 4, 4), :, columns_of(i)].reshape(256, LANES)
                    slot_buf[p][pl.ds(c * 4, 4), :, columns_of(i)] = dot(order, block).astype(jnp.bfloat16).reshape(4, 64, LANES)
                return carry

            lax.fori_loop(0, WIDTHS[p] // LANES, straighten, 0)
        block = held[...].reshape(512, WIDTHS[p])
        deep = slice(OFFSETS[p], OFFSETS[p] + WIDTHS[p])
        for n in range(2):
            for base, buf in ((0, gate_buf), (512, up_buf)):
                product = dot(block, buf[deep, n * 256 : n * 256 + 256])
                columns = slice(base + n * 256, base + n * 256 + 256)
                if p == 0:
                    acc[:, columns] = product
                else:
                    acc[:, columns] += product

    def activate(i, carry):
        rows = pl.ds(pl.multiple_of(i * 64, 64), 64)
        gate_val = acc[rows, 0:512]
        hid[rows, :] = ((gate_val / (1.0 + jnp.exp(-gate_val))) * acc[rows, 512:1024]).astype(jnp.bfloat16)
        return carry

    begin(rings_one, GROUP_A)
    begin(rings_one, GROUP_B)
    for load in loads:
        load.start()
    lax.fori_loop(0, 1, attend, 0)
    turn_round(rings_one, GROUP_A)
    turn_round(rings_one, GROUP_B)
    lax.fori_loop(1, 2, attend, 0)
    for p in GROUP_A + GROUP_B:
        finish(rings_one, p)
        begin(rings_two, (p,))
    lax.fori_loop(2, 5, attend, 0)
    turn_round(rings_two, GROUP_A)
    lax.fori_loop(5, 6, attend, 0)
    turn_round(rings_two, GROUP_B)
    for p in GROUP_A:
        spread(p)
    lax.fori_loop(6, 8, attend, 0)
    for p in GROUP_A:
        relay(p)
    for p in GROUP_B:
        spread(p)
    loads[0].wait()
    loads[1].wait()
    for p in GROUP_A:
        collect(p)
        widen(p)
        relay(p + 3)
    for p in GROUP_B:
        collect(p)
        widen(p)
    loads[2].wait()
    lax.fori_loop(0, 8, activate, 0)

    returned = []

    def give(copy):
        copy.start()
        returned.append(copy)

    def narrow(p):
        _, _, d3 = ORDERS[p]
        if d3 == 2:
            hid_p[...] = hid[...]
        else:
            order = jnp.where(source_row(p, iota((256, 256), 1)) == iota((256, 256), 0), 1.0, 0.0).astype(jnp.bfloat16)
            for c in range(2):
                hid_p[c * 256 : c * 256 + 256, :] = dot(order, hid[c * 256 : c * 256 + 256, :]).astype(jnp.bfloat16)

        def shrink(i, carry):
            deep = pl.ds(pl.multiple_of(OFFSETS[p] + i * LANES, LANES), LANES)
            recv_buf[p][:, :, columns_of(i)] = dot(hid_p[...], down_buf[:, deep]).astype(jnp.bfloat16).reshape(8, 64, LANES)
            return carry

        lax.fori_loop(0, WIDTHS[p] // LANES, shrink, 0)

    def send_back(p):
        _, _, d3 = ORDERS[p]
        here = pos[d3]
        far = (here + 2) % 4
        entry = here * 2 + core
        step = turn if d3 != 1 else pair
        for c in range(2):
            give(remote(recv_buf[p].at[c * 4 + far], relay_out[p].at[c], p, 24 + c, 28 + c, device(moved(d3, step), core)))
        for delta, base in ((1, 20), (-1, 22)):
            there = (here + delta) % 4
            for c in range(2):
                give(remote(recv_buf[p].at[c * 4 + there], back_buf[p].at[entry], p, base + c, 20 + entry, device(moved(d3, delta), c)))
        give(remote(recv_buf[p].at[(1 - core) * 4 + here], back_buf[p].at[entry], p, 26, 20 + entry, device(pos, 1 - core)))
        local[p] = pltpu.make_async_copy(recv_buf[p].at[core * 4 + here], back_buf[p].at[entry], own_sem.at[2 * PIECES + p])
        local[p].start()

    def relay_back(p):
        _, _, d3 = ORDERS[p]
        here = pos[d3]
        step = turn if d3 != 1 else -pair
        origin = -turn if d3 != 1 else pair
        entry = ((here + origin) % 4) * 2 + core
        for c in range(2):
            arrived(relay_out[p].at[c], p, 28 + c)
            give(remote(relay_out[p].at[c], back_buf[p].at[entry], p, 28 + c, 20 + entry, device(moved(d3, step), c)))

    def low_of(p, ref):
        return ref.at[(slice(None),) * (len(ref.shape) - 1) + (pl.ds(0, WIDTHS[p] // 2),)]

    def high_of(p, ref):
        return ref.at[(slice(None),) * (len(ref.shape) - 1) + (pl.ds(WIDTHS[p] // 2, WIDTHS[p] // 2),)]

    def fold(p, dim, base, late, block, bufs):
        half = WIDTHS[p] // 2
        rest = half
        here, up, down, far = pos[dim], (pos[dim] + 1) % 4, (pos[dim] + 3) % 4, (pos[dim] + 2) % 4
        above, below = device(moved(dim, 1), core), device(moved(dim, -1), core)
        low_part = lambda i: block(i, pl.ds(0, half))
        high_part = lambda i: block(i, pl.ds(half, rest))
        first = [
            remote(low_part(far), bufs[0], p, base, base, above),
            remote(high_part(far), bufs[1], p, base + 1, base + 1, below),
            remote(high_part(up), high_of(p, bufs[2]), p, late, late, above),
            remote(low_part(down), low_of(p, bufs[3]), p, late + 1, late + 1, below),
        ]
        second = [
            remote(low_part(up), low_of(p, bufs[2]), p, base + 2, base + 2, above),
            remote(high_part(down), high_of(p, bufs[3]), p, base + 3, base + 3, below),
        ]
        return first, second, low_part(up), high_part(down)

    folds_two, folds_one = [None] * PIECES, [None] * PIECES

    def merge(p):
        d1, d2, d3 = ORDERS[p]
        here = pos[d3]
        arrivals = [(here * 2 + 1 - core)]
        for delta in (1, 2, 3):
            for which in range(2):
                arrivals.append(((here + delta) % 4) * 2 + which)
        for entry in arrivals:
            arrived(back_buf[p].at[entry], p, 20 + entry)
        local[p].wait()
        near = ((iota((256, 512), 1) & 63) >> 1) == (iota((256, 512), 0) >> 3)
        mixer = jnp.where(near, dot_nt(table_of(p), chooser(p)), 0.0).astype(jnp.bfloat16)

        def mix(i, carry):
            block = back_buf[p][:, :, columns_of(i)].reshape(512, LANES)
            part_buf[p][:, :, :, columns_of(i)] = dot(mixer, block).astype(jnp.bfloat16).reshape(4, 4, 16, LANES)
            return carry

        lax.fori_loop(0, WIDTHS[p] // LANES, mix, 0)
        block_two = lambda i, columns=slice(None): part_buf[p].at[:, i, :, columns]
        block_one = lambda i, columns=slice(None): part_buf[p].at[i, pos[d2], :, columns]
        folds_two[p] = fold(p, d2, 30, 42, block_two, (wide_a[p], wide_b[p], wide_c[p], wide_d[p]))
        folds_one[p] = fold(p, d1, 34, 44, block_one, (thin_a[p], thin_b[p], thin_c[p], thin_d[p]))
        for copy in folds_two[p][0]:
            give(copy)

    def add_into(ref, *others):
        total = ref[...].astype(jnp.float32)
        for other in others:
            total = total + other[...].astype(jnp.float32)
        ref[...] = total.astype(jnp.bfloat16)

    def halfway(p, folds, base, low_buf, high_buf):
        _, second, low_up, high_down = folds[p]
        arrived(low_buf[p], p, base)
        add_into(low_up, low_buf[p])
        give(second[0])
        arrived(high_buf[p], p, base + 1)
        add_into(high_down, high_buf[p])
        give(second[1])

    def gather_sums(p, from_below, from_above, base, late):
        arrived(high_of(p, from_below), p, late)
        arrived(low_of(p, from_above), p, late + 1)
        arrived(low_of(p, from_below), p, base + 2)
        arrived(high_of(p, from_above), p, base + 3)

    def close_two(p):
        gather_sums(p, wide_c[p], wide_d[p], 30, 42)
        add_into(part_buf[p].at[:, pos[ORDERS[p][1]]], wide_c[p], wide_d[p])
        for copy in folds_one[p][0]:
            give(copy)

    outs = []

    def close_one(p):
        d1, d2, _ = ORDERS[p]
        gather_sums(p, thin_c[p], thin_d[p], 34, 44)
        total = part_buf[p][pos[d1], pos[d2]].astype(jnp.float32)
        total = total + thin_c[p][...].astype(jnp.float32) + thin_d[p][...].astype(jnp.float32)
        columns = pl.ds(OFFSETS[p], WIDTHS[p])
        out_buf[:, columns] = total.astype(jnp.bfloat16)
        outs.append(pltpu.make_async_copy(out_buf.at[:, columns], out_ref.at[:, columns], out_sem.at[p]))
        outs[-1].start()

    for p in GROUP_A:
        narrow(p)
        send_back(p)
    for p in GROUP_B:
        narrow(p)
    for p in GROUP_A:
        relay_back(p)
    for p in GROUP_B:
        send_back(p)
    drain(rings_one)
    drain(rings_two)
    for step in (6, 7):
        o_copy(step, step % 2).wait()
    for p in GROUP_A:
        merge(p)
    for p in GROUP_B:
        relay_back(p)
    slots_sent = len(returned)
    for p in GROUP_A:
        halfway(p, folds_two, 30, wide_a, wide_b)
    for p in GROUP_B:
        merge(p)
    for p in GROUP_A:
        close_two(p)
    for copy in returned[:slots_sent]:
        copy.wait_send()
    for p in GROUP_B:
        halfway(p, folds_two, 30, wide_a, wide_b)
    sums_sent = len(returned)
    for p in GROUP_A:
        halfway(p, folds_one, 34, thin_a, thin_b)
    for p in GROUP_B:
        close_two(p)
    for copy in returned[slots_sent:sums_sent]:
        copy.wait_send()
    for p in GROUP_A:
        close_one(p)
    for p in GROUP_B:
        halfway(p, folds_one, 34, thin_a, thin_b)
    for p in GROUP_B:
        close_one(p)
    for copy in returned[sums_sent:]:
        copy.wait_send()
    for copy in outs:
        copy.wait()


def hand_over(att_in, out_in, att_out, out_out, att_buf, out_buf, in_sem, out_sem):
    parts = [(out_in, out_buf, out_out)]
    for i in range(4):
        rows = pl.ds(i * 4, 4)
        parts.append((att_in.at[rows], att_buf.at[rows], att_out.at[rows]))
    takes = [pltpu.make_async_copy(a, b, in_sem.at[i]) for i, (a, b, _) in enumerate(parts)]
    gives = [pltpu.make_async_copy(b, c, out_sem.at[i]) for i, (_, b, c) in enumerate(parts)]
    for take in takes:
        take.start()
    for take, give in zip(takes, gives):
        take.wait()
        give.start()
    for give in gives:
        give.wait()


def per_device(
    hidden_in,
    expert_ids,
    gate_coef,
    query_lat,
    kv_cache,
    cache_len,
    gate_weight,
    up_weight,
    down_weight,
):
    bf16, f32 = jnp.bfloat16, jnp.float32
    vmem = lambda *shape, dtype=bf16: pltpu.VMEM(shape, dtype)
    dma = pltpu.SemaphoreType.DMA
    scratch = (
        [vmem(4, 4, 16, w + e) for w, e in zip(WIDTHS, EXTRA)]
        + [vmem(8, 64, w) for w in WIDTHS]
        + [vmem(8, 64, w) for w in WIDTHS]
        + [vmem(8, 64, w) for w in WIDTHS]
        + [vmem(2, 64, w) if o[2] != 1 else vmem(2, 64, 128) for o, w in zip(ORDERS, WIDTHS)]
        + [vmem(2, 64, w) for w in WIDTHS]
        + [vmem(4, 4, 16, w) for w in WIDTHS]
        + [vmem(4, 16, w // 2) for w in WIDTHS] * 2
        + [vmem(4, 16, w) for w in WIDTHS] * 2
        + [vmem(16, w // 2) for w in WIDTHS] * 2
        + [vmem(16, w) for w in WIDTHS] * 2
        + [
            vmem(7168, 512),
            vmem(7168, 512),
            vmem(512, 7168),
            vmem(512, 1024, dtype=f32),
            vmem(512, 512),
            vmem(512, 512),
            vmem(2, 2, 64, 576),
            vmem(2, 2, 576, 128),
            vmem(2, 2, 64, 512),
            dma((PIECES, 46)),
            dma((PIECES, 46)),
            dma((3,)),
            dma((3 * PIECES,)),
            dma((2,)),
            dma((2,)),
            dma((2,)),
            pltpu.SMEM((16,), jnp.int32),
            vmem(8, 16, dtype=jnp.int32),
            vmem(8, 16, dtype=f32),
            vmem(16, 7168),
            dma((PIECES,)),
            dma((3,)),
        ]
    )
    anywhere = pl.BlockSpec(memory_space=pl.ANY)
    attention, routed = pl.pallas_call(
        kernel,
        out_shape=(
            jax.ShapeDtypeStruct((16, 64, 512), bf16),
            jax.ShapeDtypeStruct((16, 7168), bf16),
        ),
        in_specs=[anywhere] * 9,
        out_specs=(anywhere, anywhere),
        scratch_shapes=scratch,
        compiler_params=pltpu.CompilerParams(
            collective_id=0, has_side_effects=True, vmem_limit_bytes=67043328
        ),
        name="moe_step",
    )(
        cache_len,
        expert_ids.T,
        gate_coef.T,
        hidden_in,
        query_lat,
        jnp.swapaxes(kv_cache, 1, 2),
        gate_weight,
        up_weight,
        down_weight,
    )
    return pl.pallas_call(
        hand_over,
        out_shape=(
            jax.ShapeDtypeStruct((16, 64, 512), bf16),
            jax.ShapeDtypeStruct((16, 7168), bf16),
        ),
        in_specs=[anywhere] * 2,
        out_specs=(anywhere, anywhere),
        scratch_shapes=[vmem(16, 64, 512), vmem(16, 7168), dma((5,)), dma((5,))],
        name="hand_over",
    )(attention, routed)


def solution(mesh):
    in_specs = (
        P(("sec", "dev"), None),
        P(("sec", "dev"), None),
        P(("sec", "dev"), None),
        P(("sec", "dev"), None, None),
        P(("sec", "dev"), None, None),
        P(("sec", "dev")),
        P("dev", None, "sec"),
        P("dev", None, "sec"),
        P("dev", "sec", None),
    )
    out_specs = (P(("sec", "dev"), None, None), P(("sec", "dev"), None))
    return jax.shard_map(
        per_device, mesh=mesh, in_specs=in_specs, out_specs=out_specs, check_vma=False
    )
```
